32 devices in a mesh: fsdp: 4 (over z), ctx: 4 (over y, x), tp: 2 (over core).
Axes of the slice: x: 2, y: 2, z: 4, core: 2. Of those that a mesh axis runs over, the one named last changes fastest.
Arguments:
- tokens: bfloat16 [16384, 2048], P(('fsdp', 'ctx')), may hold values from -6 to 6
- cotangent: bfloat16 [16384, 2048], P(('fsdp', 'ctx')), may hold values from -6 to 6
- routes: int32 [16384, 8], P(('fsdp', 'ctx')), may hold values from 0 to 15, all different within a row; in each aligned block of 1024 rows (0 to 1023, 1024 to 2047, ...) at most 576 rows name the same one
- adapter_ids: int32 [4, 9], P('fsdp'), may hold values from 0 to 7
- norm_in: bfloat16 [2048], replicated, may hold values from 0.5 to 1.5
- norm_mid: bfloat16 [2048], replicated, may hold values from 0.5 to 1.5
- q_gain: bfloat16 [2048], P('tp'), may hold values from 1 to 2
- k_gain: bfloat16 [2048], P('tp'), may hold values from 1 to 2
- w_qkv: bfloat16 [2048, 3, 2048], P('fsdp', None, 'tp'), may hold values from -0.125 to 0.125
- w_out: bfloat16 [2048, 2048], P('tp', 'fsdp'), may hold values from -0.375 to 0.375
- w_router: bfloat16 [2048, 16], replicated, may hold values from -0.0625 to 0.0625
- w_gate_up: bfloat16 [16, 2048, 2, 1024], P('fsdp', None, None, 'tp'), may hold values from -0.125 to 0.125
- w_down: bfloat16 [16, 1024, 2048], P('fsdp', 'tp'), may hold values from -1.5 to 1.5
- qkv_a: bfloat16 [8, 2048, 3, 16], P('fsdp'), may hold values from -0.125 to 0.125
- qkv_b: bfloat16 [8, 16, 3, 2048], P('fsdp', None, None, 'tp'), may hold values from -1.5 to 1.5
- out_a: bfloat16 [8, 2048, 16], P('fsdp', 'tp'), may hold values from -0.125 to 0.125
- out_b: bfloat16 [8, 16, 2048], P('fsdp'), may hold values from -4 to 4
- router_a: bfloat16 [8, 2048, 16], P('fsdp'), may hold values from -0.125 to 0.125
- router_b: bfloat16 [8, 16, 16], P('fsdp'), may hold values from -0.75 to 0.75
- gu_a: bfloat16 [8, 16, 2048, 2, 16], P('fsdp'), may hold values from -0.125 to 0.125
- gu_b: bfloat16 [8, 16, 16, 2, 1024], P('fsdp', None, None, None, 'tp'), may hold values from -1.5 to 1.5
- down_a: bfloat16 [8, 16, 1024, 16], P('fsdp', None, 'tp'), may hold values from -0.1875 to 0.1875
- down_b: bfloat16 [8, 16, 16, 2048], P('fsdp'), may hold values from -6 to 6
Outputs:
- mixed: bfloat16 [16384, 2048], P(('fsdp', 'ctx'))
- grad_input: float32 [16384, 2048], P(('fsdp', 'ctx'))
- grad_qkv_a: float32 [8, 2048, 3, 16], P('fsdp')
- grad_qkv_b: float32 [8, 16, 3, 2048], P('fsdp', None, None, 'tp')
- grad_out_a: float32 [8, 2048, 16], P('fsdp', 'tp')
- grad_out_b: float32 [8, 16, 2048], P('fsdp')
- grad_router_a: float32 [8, 2048, 16], P('fsdp')
- grad_router_b: float32 [8, 16, 16], P('fsdp')
- grad_gu_a: float32 [8, 16, 2048, 2, 16], P('fsdp')
- grad_gu_b: float32 [8, 16, 16, 2, 1024], P('fsdp', None, None, None, 'tp')
- grad_down_a: float32 [8, 16, 1024, 16], P('fsdp', None, 'tp')
- grad_down_b: float32 [8, 16, 16, 2048], P('fsdp')
The draws below stay inside these ranges and needn't reach their ends.
Inputs may be any that keep to these rules, and one draw needn't show every extreme that they name: `routes`: each row names 8 different experts. In the rows of one device (each aligned block of 1024 rows) no expert is named by more than 576 rows, and in some block some expert is named by exactly 576 rows.
All inputs are finite; a program needn't handle non-finite values.
Results may differ from the reference program's by a relative error of at most 0.023.
Values may be sent and summed in bfloat16 or wider, within the bound.
No kernel may reach another device: no remote copies, remote signals or barrier semaphores. Data moves between devices by JAX's collectives and lax.ppermute only.
A program may use at most 576 MiB of HBM per device.

```python
import math
import jax
import jax.numpy as jnp
import numpy as np
from jax import lax

D = 2048
HEADS = 16
HEAD_DIM = 128
FF = 1024
TOPK = 8
EXPERTS = 16
SETS = 8
RANK = 16
PROMPT = 2048
CONT_LEN = 256
CONTS = 8
SLABS = 4
PROMPT_DEV = 512
CONT_DEV = 2
ROWS_DEV = 1024
GROUPS = 4
TOKENS = 16384
CAP = 576


def set_ends(entries, stream_key, low, high):
    dims = entries.shape
    spot = [jax.random.randint(jax.random.fold_in(stream_key, axis), (), 0, dims[axis]) for axis in range(len(dims))]
    entries = entries.at[tuple(spot)].set(low)
    longest = dims.index(max(dims))
    spot[longest] = (spot[longest] + 1) % dims[longest]
    return entries.at[tuple(spot)].set(high)


def steps_of(stream_key, extent, cuts, smallest, high):
    level = 1.0
    for axis_at, shards_of in cuts:
        steps = jax.random.uniform(jax.random.fold_in(jax.random.fold_in(stream_key, 6), axis_at), (shards_of,), jnp.float32, smallest / len(cuts), high / len(cuts))
        level = level * jnp.repeat(jnp.exp(steps), extent[axis_at] // shards_of).reshape((-1,) + (1,) * (len(extent) - 1 - axis_at))
    return level


def routed_block(own_key, own, number, rows, amount, top, limit, lean):
    ranking = jax.random.permutation(own_key, amount)
    crowded, ordinary = portions_of(amount, rows * top, limit, lean, True), portions_of(amount, rows * top, limit, lean, False)
    places = jnp.arange(amount)

    def named(sizes, turn):
        used = int((sizes > 0).sum())
        fixed = max(1, used // 4)
        moved = fixed + (places - fixed + turn * (used - fixed)) % max(1, amount - fixed)
        return jnp.zeros((amount,), jnp.int32).at[ranking[jnp.where(places < fixed, places, moved)]].set(jnp.asarray(sizes, jnp.int32))

    sizes = jnp.where(number % 4 == 0, named(crowded, number // 4), named(ordinary, number - number // 4 - 1))
    mixed = jax.random.permutation(jax.random.fold_in(own, 3), amount)
    donor, sink = mixed[0:amount // 2 * 2:2], mixed[1:amount // 2 * 2:2]
    room = jnp.minimum(sizes[donor] - 1, limit - sizes[sink]) // 2
    room = jnp.where((donor == ranking[0]) | (sink == ranking[0]) | (sizes[sink] == 0), 0, jnp.maximum(room, 0))
    moved = jax.random.randint(jax.random.fold_in(own, 4), (amount // 2,), 0, 1 << 20) % (room + 1)
    sizes = sizes.at[donor].add(-moved).at[sink].add(moved)
    labels = jnp.searchsorted(jnp.cumsum(sizes), jnp.arange(rows * top), side="right").astype(jnp.int32)
    listing = labels.reshape(top, rows).T
    listing = listing[jax.random.permutation(jax.random.fold_in(own, 1), rows)]
    turn = jax.random.randint(jax.random.fold_in(own, 2), (rows, 1), 0, top)
    return jnp.take_along_axis(listing, (jnp.arange(top)[None, :] + turn) % top, axis=1)


def portions_of(count, total, most, skew, full):
    loads = [(1 << 20) // math.isqrt(grade ** skew) + 1 for grade in range(1, count + 1)]
    largest = most if full else min(most, max(-(-total // count), total * loads[0] // sum(loads)))
    least = 1 if total - largest >= count - 1 else 0
    counts, spare = [largest] + [least] * (count - 1), total - largest - least * (count - 1)
    while spare > 0:
        free = [i for i in range(1, count) if counts[i] < largest] or [i for i in range(1, count) if counts[i] < most]
        mass, budget = sum([loads[i] for i in free]), spare
        for i in free:
            more = min(most - counts[i], max(1, budget * loads[i] // mass), spare)
            counts[i] = counts[i] + more
            spare = spare - more
    return np.array(counts)


def gaussian(rng, extent, scale, most, shards=(), held_as=jnp.bfloat16):
    entries = scale * jax.random.normal(rng, extent, jnp.float32)
    if shards:
        entries = entries * steps_of(rng, extent, shards, -0.22, 0.18)
    return jnp.clip(entries, -most, most).astype(held_as)


def setup_inputs(seed: int = 0) -> dict:
    keys = jax.random.split(jax.random.key(seed), 24)
    tokens = gaussian(keys[0], (TOKENS, D), 1.0, 6.0, ((0, 16),))
    cotangent = gaussian(keys[1], (TOKENS, D), 1.0, 6.0, ((0, 16),))
    routes_keys = jax.random.split(jax.random.fold_in(keys[2], 1), TOKENS // ROWS_DEV)
    routes_turns = jax.random.permutation(jax.random.fold_in(keys[2], 3), TOKENS // ROWS_DEV)
    routes = jax.vmap(lambda own, number: routed_block(jax.random.fold_in(keys[2], 2), own, number, ROWS_DEV, EXPERTS, TOPK, CAP, 1))(routes_keys, routes_turns).reshape((TOKENS, TOPK))
    adapter_ids = set_ends(jax.random.randint(keys[3], (GROUPS, CONTS + 1), 0, SETS), jax.random.fold_in(keys[3], 1), 0, SETS - 1).astype(jnp.int32)
    norm_in = jnp.clip(1.0 + 0.1 * jax.random.normal(keys[4], (D,), jnp.float32), 0.5, 1.5).astype(jnp.bfloat16)
    norm_mid = jnp.clip(1.0 + 0.1 * jax.random.normal(keys[5], (D,), jnp.float32), 0.5, 1.5).astype(jnp.bfloat16)
    q_gain = jnp.clip(1.0 + 1.0 * jax.random.uniform(keys[6], (D,), jnp.float32) ** steps_of(keys[6], (D,), ((0, 2),), -0.2, 0.2), 1.0, 2.0).astype(jnp.bfloat16)
    k_gain = jnp.clip(1.0 + 1.0 * jax.random.uniform(keys[7], (D,), jnp.float32) ** steps_of(keys[7], (D,), ((0, 2),), -0.2, 0.2), 1.0, 2.0).astype(jnp.bfloat16)
    w_qkv = gaussian(keys[8], (D, 3, D), D ** -0.5, 0.125, ((0, 4), (2, 2)))
    w_out = gaussian(keys[9], (D, D), (D // 8) ** -0.5, 0.375, ((0, 2), (1, 4)))
    w_router = gaussian(keys[10], (D, EXPERTS), (4 * D) ** -0.5, 0.0625)
    w_gate_up = gaussian(keys[11], (EXPERTS, D, 2, FF), D ** -0.5, 0.125, ((0, 4), (3, 2)))
    w_down = gaussian(keys[12], (EXPERTS, FF, D), (max(FF // 64, 1)) ** -0.5, 1.5, ((0, 4), (1, 2)))
    qkv_a = gaussian(keys[13], (SETS, D, 3, RANK), D ** -0.5, 0.125, ((0, 4),))
    qkv_b = gaussian(keys[14], (SETS, RANK, 3, D), RANK ** -0.5, 1.5, ((0, 4), (3, 2)))
    out_a = gaussian(keys[15], (SETS, D, RANK), D ** -0.5, 0.125, ((0, 4), (1, 2)))
    out_b = gaussian(keys[16], (SETS, RANK, D), (max(RANK // 8, 1)) ** -0.5, 4.0, ((0, 4),))
    router_a = gaussian(keys[17], (SETS, D, RANK), D ** -0.5, 0.125, ((0, 4),))
    router_b = gaussian(keys[18], (SETS, RANK, EXPERTS), (4 * RANK) ** -0.5, 0.75, ((0, 4),))
    gu_a = gaussian(keys[19], (SETS, EXPERTS, D, 2, RANK), D ** -0.5, 0.125, ((0, 4),))
    gu_b = gaussian(keys[20], (SETS, EXPERTS, RANK, 2, FF), RANK ** -0.5, 1.5, ((0, 4), (4, 2)))
    down_a = gaussian(keys[21], (SETS, EXPERTS, FF, RANK), FF ** -0.5, 0.1875, ((0, 4), (2, 2)))
    down_b = gaussian(keys[22], (SETS, EXPERTS, RANK, D), (max(RANK // 16, 1)) ** -0.5, 6.0, ((0, 4),))
    return dict(tokens=tokens, cotangent=cotangent, routes=routes, adapter_ids=adapter_ids, norm_in=norm_in, norm_mid=norm_mid, q_gain=q_gain, k_gain=k_gain, w_qkv=w_qkv, w_out=w_out, w_router=w_router, w_gate_up=w_gate_up, w_down=w_down, qkv_a=qkv_a, qkv_b=qkv_b, out_a=out_a, out_b=out_b, router_a=router_a, router_b=router_b, gu_a=gu_a, gu_b=gu_b, down_a=down_a, down_b=down_b)


epsilon = 1e-05
ADAPTER_SCALE = 0.5
ROPE_BASE = 10000.0
masked_score = -1e+30
highest_precision = lax.Precision.HIGHEST

@jax.custom_vjp
def low(v):
    return lax.optimization_barrier(v.astype(jnp.bfloat16)).astype(jnp.float32)

@jax.custom_vjp
def adapter_backward(v):
    return v

def low_keep(v):
    return (low(v), None)

def low_pass(kept, grad):
    return (grad,)

def back_keep(v):
    return (v, None)

def back_low(kept, grad):
    return (low(grad),)
low.defvjp(low_keep, low_pass)
adapter_backward.defvjp(back_keep, back_low)

def rms_scale(value, gain):
    return value * lax.rsqrt(lax.optimization_barrier(jnp.mean(value * value, axis=-1, keepdims=True)) + epsilon) * gain

def angles(positions):
    freqs = ROPE_BASE ** (-(2.0 * jnp.arange(HEAD_DIM // 2, dtype=jnp.float32)) / HEAD_DIM)
    turned = positions.astype(jnp.float32)[:, None] * freqs[None, :]
    return (jnp.cos(turned)[:, None, :], jnp.sin(turned)[:, None, :])

def rotate(value, cosine, sine_part):
    half_dim = value.shape[-1] // 2
    first_half = value[..., :half_dim]
    second_half = value[..., half_dim:]
    return jnp.concatenate([first_half * cosine - second_half * sine_part, second_half * cosine + first_half * sine_part], axis=-1)

def layout():
    row_index = jnp.arange(ROWS_DEV, dtype=jnp.int32)[None, :]
    slab_index = jnp.arange(SLABS, dtype=jnp.int32)[:, None]
    tail_offset = jnp.maximum(row_index - PROMPT_DEV, 0)
    leading = row_index < PROMPT_DEV
    positions = jnp.where(leading, slab_index * PROMPT_DEV + row_index, PROMPT + tail_offset % CONT_LEN)
    sequence = jnp.where(leading, 0, 1 + slab_index * CONT_DEV + tail_offset // CONT_LEN)
    return (positions.reshape(-1).astype(jnp.int32), sequence.reshape(-1).astype(jnp.int32))

def split_tokens(value):
    rest = value.shape[1:]
    value = value.reshape((SLABS, ROWS_DEV) + rest)
    prompt_part = value[:, :PROMPT_DEV].reshape((PROMPT,) + rest)
    cont_part = value[:, PROMPT_DEV:].reshape((CONTS, CONT_LEN) + rest)
    return (prompt_part, cont_part)

def join_tokens(prompt_part, cont_part):
    rest = prompt_part.shape[1:]
    prompt_part = prompt_part.reshape((SLABS, PROMPT_DEV) + rest)
    cont_part = cont_part.reshape((SLABS, CONT_DEV * CONT_LEN) + rest)
    return jnp.concatenate([prompt_part, cont_part], axis=1).reshape((SLABS * ROWS_DEV,) + rest)

def adapter_single_apply(hidden_state, adapter_down_factor, adapter_up_factor, adapter_selector):
    middle_rows = jnp.einsum('td,sdr->tsr', hidden_state, adapter_down_factor, precision=highest_precision) * adapter_selector[:, :, None]
    return ADAPTER_SCALE * jnp.einsum('hxj,xji->hi', middle_rows, adapter_up_factor, precision=highest_precision)

def adapter_stacked_apply(hidden_state, adapter_down_factor, adapter_up_factor, adapter_selector):
    middle_rows = jnp.einsum('td,sdjr->tsjr', hidden_state, adapter_down_factor, precision=highest_precision) * adapter_selector[:, :, None, None]
    return ADAPTER_SCALE * jnp.einsum('ladi,aidv->ldv', middle_rows, adapter_up_factor, precision=highest_precision)

def head_attention(query_head, key_head, value_head):
    score_scale = HEAD_DIM ** (-0.5)
    query_p, query_c = split_tokens(query_head)
    key_p, key_c = split_tokens(key_head)
    value_p, value_c = split_tokens(value_head)
    prompt_idx = jnp.arange(PROMPT, dtype=jnp.int32)
    cont_idx = jnp.arange(CONT_LEN, dtype=jnp.int32)
    prompt_scores = adapter_backward(jnp.einsum('qd,kd->qk', query_p, key_p, precision=highest_precision) * score_scale)
    prompt_scores = jnp.where(prompt_idx[:, None] >= prompt_idx[None, :], prompt_scores, masked_score)
    prompt_probs = low(jax.nn.softmax(prompt_scores, axis=-1))
    prompt_out = jnp.einsum('qk,kd->qd', prompt_probs, value_p, precision=highest_precision)
    front = jnp.einsum('cqd,kd->cqk', query_c, key_p, precision=highest_precision) * score_scale
    behind = jnp.einsum('cqd,ckd->cqk', query_c, key_c, precision=highest_precision) * score_scale
    cont_scores = adapter_backward(jnp.concatenate([front, behind], axis=-1))
    allowed = jnp.concatenate([jnp.ones((CONT_LEN, PROMPT), dtype=bool), cont_idx[:, None] >= cont_idx[None, :]], axis=1)
    cont_scores = jnp.where(allowed[None], cont_scores, masked_score)
    cont_probs = low(jax.nn.softmax(cont_scores, axis=-1))
    cont_out = jnp.einsum('cqk,kd->cqd', cont_probs[..., :PROMPT], value_p, precision=highest_precision)
    cont_out = cont_out + jnp.einsum('cqk,ckd->cqd', cont_probs[..., PROMPT:], value_c, precision=highest_precision)
    return join_tokens(prompt_out, cont_out)

def attend_head(step_input):
    return head_attention(step_input[0], step_input[1], step_input[2])

def expert_term(hidden_after_experts, adapter_selector, expert_gate_up_weight, expert_down_weight, gate_up_first_factor, gate_up_second_factor, expert_down_first_factor, expert_down_second_factor):
    gate_up_rows = jnp.einsum('fn,nqc->fqc', hidden_after_experts, expert_gate_up_weight, precision=highest_precision) + adapter_stacked_apply(hidden_after_experts, gate_up_first_factor, gate_up_second_factor, adapter_selector)
    gate_up_rows = adapter_backward(gate_up_rows)
    hidden_state = low(jax.nn.silu(gate_up_rows[:, 0]) * gate_up_rows[:, 1])
    expert_output_rows = jnp.dot(hidden_state, expert_down_weight, precision=highest_precision) + adapter_single_apply(hidden_state, expert_down_first_factor, expert_down_second_factor, adapter_selector)
    return adapter_backward(expert_output_rows)

def reference(tokens, cotangent, routes, adapter_ids, norm_in, norm_mid, q_gain, k_gain, w_qkv, w_out, w_router, w_gate_up, w_down, qkv_a, qkv_b, out_a, out_b, router_a, router_b, gu_a, gu_b, down_a, down_b):
    per_group = SLABS * ROWS_DEV
    positions, sequence = layout()
    cosine, sine_part = angles(positions)
    gain_in = norm_in.astype(jnp.float32)
    gain_mid = norm_mid.astype(jnp.float32)
    gain_q = q_gain.astype(jnp.float32)
    gain_k = k_gain.astype(jnp.float32)
    query_key_value_weight = w_qkv.astype(jnp.float32)
    output_weight = w_out.astype(jnp.float32)
    router_weight = w_router.astype(jnp.float32)
    gate_up_w = w_gate_up.astype(jnp.float32)
    down_w = w_down.astype(jnp.float32)

    def group_layer(adapters, group_tokens, group_routes, group_ids):
        projection_down_factor, projection_up_factor, output_down_factor, output_up_factor, router_down_factor, router_up_factor, a_gu, b_gu, a_down, b_down = adapters
        adapter_selector = (group_ids[sequence][:, None] == jnp.arange(SETS, dtype=jnp.int32)[None, :]).astype(jnp.float32)
        hidden_after_attention = low(rms_scale(group_tokens, gain_in))
        projection_rows = adapter_backward(jnp.einsum('yp,pma->yma', hidden_after_attention, query_key_value_weight, precision=highest_precision) + adapter_stacked_apply(hidden_after_attention, projection_down_factor, projection_up_factor, adapter_selector))
        queries = low(rotate(rms_scale(projection_rows[:, 0], gain_q).reshape(per_group, HEADS, HEAD_DIM), cosine, sine_part))
        key_vals = low(rotate(rms_scale(projection_rows[:, 1], gain_k).reshape(per_group, HEADS, HEAD_DIM), cosine, sine_part))
        value_vals = low(projection_rows[:, 2]).reshape(per_group, HEADS, HEAD_DIM)
        heads_out = lax.map(jax.checkpoint(attend_head), (jnp.moveaxis(queries, 1, 0), jnp.moveaxis(key_vals, 1, 0), jnp.moveaxis(value_vals, 1, 0)))
        attention_result = low(adapter_backward(jnp.moveaxis(heads_out, 0, 1).reshape(per_group, D)))
        adapter_branch = adapter_backward(jnp.dot(attention_result, output_weight, precision=highest_precision) + adapter_single_apply(attention_result, output_down_factor, output_up_factor, adapter_selector))
        x_mid = group_tokens + adapter_branch
        hidden_after_experts = low(rms_scale(x_mid, gain_mid))
        router_logits = adapter_backward(jnp.dot(hidden_after_experts, router_weight, precision=highest_precision) + adapter_single_apply(hidden_after_experts, router_down_factor, router_up_factor, adapter_selector))
        expert_probs = jax.nn.softmax(router_logits, axis=-1)
        chosen = (group_routes[:, :, None] == jnp.arange(EXPERTS, dtype=jnp.int32)[None, None, :]).astype(jnp.float32)
        combine_w = lax.optimization_barrier(jnp.sum(chosen * expert_probs[:, None, :], axis=1))

        def expert_step(running, step_input):
            expert_gate_up_weight, expert_down_weight, gate_up_first_factor, gate_up_second_factor, expert_down_first_factor, expert_down_second_factor, weight_col = step_input
            term = expert_term(hidden_after_experts, adapter_selector, expert_gate_up_weight, expert_down_weight, gate_up_first_factor, gate_up_second_factor, expert_down_first_factor, expert_down_second_factor)
            return (running + term * weight_col[:, None], None)
        routed_sum, unused = lax.scan(jax.checkpoint(expert_step), jnp.zeros((per_group, D), jnp.float32), (gate_up_w, down_w, jnp.moveaxis(a_gu, 1, 0), jnp.moveaxis(b_gu, 1, 0), jnp.moveaxis(a_down, 1, 0), jnp.moveaxis(b_down, 1, 0), combine_w.T))
        return x_mid + routed_sum

    def whole(token_vals, adapters):

        def group_step(carry_val, step_input):
            return (carry_val, jax.checkpoint(group_layer)(adapters, step_input[0], step_input[1], step_input[2]))
        unused, outputs = lax.scan(group_step, jnp.zeros((), jnp.float32), (token_vals.reshape(GROUPS, per_group, D), routes.reshape(GROUPS, per_group, TOPK), adapter_ids))
        return outputs.reshape(TOKENS, D)
    adapters = (qkv_a.astype(jnp.float32), qkv_b.astype(jnp.float32), out_a.astype(jnp.float32), out_b.astype(jnp.float32), router_a.astype(jnp.float32), router_b.astype(jnp.float32), gu_a.astype(jnp.float32), gu_b.astype(jnp.float32), down_a.astype(jnp.float32), down_b.astype(jnp.float32))
    mixed, pullback = jax.vjp(whole, tokens.astype(jnp.float32), adapters)
    grad_input, grad_adapters = pullback(cotangent.astype(jnp.float32))
    return (mixed.astype(jnp.bfloat16), grad_input, grad_adapters[0], grad_adapters[1], grad_adapters[2], grad_adapters[3], grad_adapters[4], grad_adapters[5], grad_adapters[6], grad_adapters[7], grad_adapters[8], grad_adapters[9])
```

```python
import jax
import jax.numpy as jnp
from jax import lax
from jax.experimental import pallas as pl
from jax.experimental.pallas import tpu as pltpu
from jax.sharding import PartitionSpec as P

HEAD_DIM = 128
TOPK = 8
EXPERTS = 16
RANK = 16
PROMPT = 2048
CONT_LEN = 256
CONTS = 8
SETS = 8

epsilon = 1e-05
ADAPTER_SCALE = 0.5
ROPE_BASE = 10000.0
masked_score = -1e30
TILE = CONT_LEN
SCORE_SCALE = HEAD_DIM ** (-0.5)
f32 = jnp.float32
bf16 = jnp.bfloat16


def dot_nn(a, b):
    return lax.dot_general(a, b, (((1,), (0,)), ((), ())), preferred_element_type=f32)


def dot_nt(a, b):
    return lax.dot_general(a, b, (((1,), (1,)), ((), ())), preferred_element_type=f32)


def dot_tn(a, b):
    return lax.dot_general(a, b, (((0,), (0,)), ((), ())), preferred_element_type=f32)


def rms_back(value, gain, grad, scale_col, full_width):
    inner = jnp.sum(gain * value * grad, axis=-1, keepdims=True)
    return (
        scale_col * gain * grad - value * (scale_col * scale_col * scale_col) * inner / full_width
    )


def angles(positions):
    freqs = ROPE_BASE ** (-(2.0 * jnp.arange(HEAD_DIM // 2, dtype=f32)) / HEAD_DIM)
    turned = positions.astype(f32)[:, None] * freqs[None, :]
    return (jnp.cos(turned)[:, None, :], jnp.sin(turned)[:, None, :])


def rotate(value, cosine, sine_part):
    half_dim = value.shape[-1] // 2
    first_half = value[..., :half_dim]
    second_half = value[..., half_dim:]
    return jnp.concatenate(
        [
            first_half * cosine - second_half * sine_part,
            second_half * cosine + first_half * sine_part,
        ],
        axis=-1,
    )


def attention_scores(k_ref, q, slab_ref, tile, prompt_rows, is_prompt):
    scores = dot_nt(k_ref[...], q) * SCORE_SCALE
    if not is_prompt:
        return scores
    key_at = lax.broadcasted_iota(jnp.int32, scores.shape, 0)
    query_at = (
        slab_ref[0] * prompt_rows + tile * TILE + lax.broadcasted_iota(jnp.int32, scores.shape, 1)
    )
    return jnp.where(key_at <= query_at, scores, masked_score)


def own_scores(ko_ref, q):
    scores = dot_nt(ko_ref[...], q) * SCORE_SCALE
    key_at = lax.broadcasted_iota(jnp.int32, scores.shape, 0)
    query_at = lax.broadcasted_iota(jnp.int32, scores.shape, 1)
    return jnp.where(key_at <= query_at, scores, masked_score)


def attention_forward(slab, q, k, v, ko, vo, prompt_rows):
    rows, width = q.shape
    heads, tiles, prompt_tiles = width // HEAD_DIM, rows // TILE, prompt_rows // TILE
    keys = k.shape[0]

    def body(slab_ref, q_ref, k_ref, v_ref, ko_ref, vo_ref, att_ref, lse_ref, vt_ref):
        tile = pl.program_id(1)

        @pl.when(tile == 0)
        def _():
            vt_ref[...] = v_ref[...].T

        query = q_ref[...]

        def finish(total, peak, out_t):
            att_ref[...] = (out_t / total).T.astype(bf16)
            lse_ref[0] = peak + jnp.log(total)

        @pl.when(tile < prompt_tiles)
        def _():
            scores = attention_scores(k_ref, query, slab_ref, tile, prompt_rows, True)
            peak = jnp.max(scores, axis=0, keepdims=True)
            probs = jnp.exp(scores - peak)
            total = jnp.sum(probs, axis=0, keepdims=True)
            finish(total, peak, dot_nn(vt_ref[...], probs.astype(bf16)))

        @pl.when(tile >= prompt_tiles)
        def _():
            scores = attention_scores(k_ref, query, slab_ref, tile, prompt_rows, False)
            own = own_scores(ko_ref, query)
            peak = jnp.maximum(
                jnp.max(scores, axis=0, keepdims=True), jnp.max(own, axis=0, keepdims=True)
            )
            probs = jnp.exp(scores - peak)
            own_probs = jnp.exp(own - peak)
            total = jnp.sum(probs, axis=0, keepdims=True) + jnp.sum(
                own_probs, axis=0, keepdims=True
            )
            out_t = dot_nn(vt_ref[...], probs.astype(bf16)) + dot_nn(
                vo_ref[...].T, own_probs.astype(bf16)
            )
            finish(total, peak, out_t)

    tile_spec = pl.BlockSpec((TILE, HEAD_DIM), lambda h, t, s: (t, h))
    key_spec = pl.BlockSpec((keys, HEAD_DIM), lambda h, t, s: (0, h))
    own_spec = pl.BlockSpec(
        (TILE, HEAD_DIM), lambda h, t, s: (jnp.maximum(t - prompt_tiles, 0), h)
    )
    return pl.pallas_call(
        body,
        grid_spec=pltpu.PrefetchScalarGridSpec(
            num_scalar_prefetch=1,
            grid=(heads, tiles),
            in_specs=[tile_spec, key_spec, key_spec, own_spec, own_spec],
            out_specs=[tile_spec, pl.BlockSpec((1, 1, TILE), lambda h, t, s: (h, 0, t))],
            scratch_shapes=[pltpu.VMEM((HEAD_DIM, keys), bf16)],
        ),
        out_shape=[
            jax.ShapeDtypeStruct((rows, width), bf16),
            jax.ShapeDtypeStruct((heads, 1, rows), f32),
        ],
        compiler_params=pltpu.CompilerParams(
            dimension_semantics=("arbitrary", "arbitrary"), vmem_limit_bytes=56 << 20
        ),
        name="attention_forward",
    )(slab, q, k, v, ko, vo)


def attention_backward(slab, q, k, v, ko, vo, att, d_att, lse, prompt_rows):
    rows, width = q.shape
    heads, tiles, prompt_tiles = width // HEAD_DIM, rows // TILE, prompt_rows // TILE
    keys = k.shape[0]

    def body(
        slab_ref, q_ref, k_ref, v_ref, ko_ref, vo_ref, att_ref, da_ref, lse_ref,
        dq_ref, dk_ref, dv_ref, dko_ref, dvo_ref, kt_ref, dka_ref, dva_ref,
    ):
        tile = pl.program_id(1)

        @pl.when(tile == 0)
        def _():
            kt_ref[...] = k_ref[...].T
            dka_ref[...] = jnp.zeros_like(dka_ref)
            dva_ref[...] = jnp.zeros_like(dva_ref)

        query = q_ref[...]
        d_out = da_ref[...]
        delta = jnp.sum(
            (d_out.astype(f32) * att_ref[...].astype(f32)).T, axis=0, keepdims=True
        )
        log_total = lse_ref[0]

        def prompt_keys(is_prompt):
            scores = attention_scores(k_ref, query, slab_ref, tile, prompt_rows, is_prompt)
            probs = jnp.exp(scores - log_total)
            d_probs = dot_nt(v_ref[...], d_out)
            d_scores = (probs * (d_probs - delta)).astype(bf16)
            dka_ref[...] += dot_nn(d_scores, query)
            dva_ref[...] += dot_nn(probs.astype(bf16), d_out)
            return dot_nn(kt_ref[...], d_scores)

        @pl.when(tile < prompt_tiles)
        def _():
            dq_ref[...] = prompt_keys(True).T * SCORE_SCALE

        @pl.when(tile >= prompt_tiles)
        def _():
            dq_t = prompt_keys(False)
            probs = jnp.exp(own_scores(ko_ref, query) - log_total)
            d_probs = dot_nt(vo_ref[...], d_out)
            d_scores = (probs * (d_probs - delta)).astype(bf16)
            dko_ref[...] = dot_nn(d_scores, query) * SCORE_SCALE
            dvo_ref[...] = dot_nn(probs.astype(bf16), d_out)
            dq_ref[...] = (dq_t + dot_nn(ko_ref[...].T, d_scores)).T * SCORE_SCALE

        @pl.when(tile == tiles - 1)
        def _():
            dk_ref[...] = (dka_ref[...] * SCORE_SCALE).astype(bf16)
            dv_ref[...] = dva_ref[...].astype(bf16)

    tile_spec = pl.BlockSpec((TILE, HEAD_DIM), lambda h, t, s: (t, h))
    key_spec = pl.BlockSpec((keys, HEAD_DIM), lambda h, t, s: (0, h))
    own_spec = pl.BlockSpec(
        (TILE, HEAD_DIM), lambda h, t, s: (jnp.maximum(t - prompt_tiles, 0), h)
    )
    return pl.pallas_call(
        body,
        grid_spec=pltpu.PrefetchScalarGridSpec(
            num_scalar_prefetch=1,
            grid=(heads, tiles),
            in_specs=[
                tile_spec, key_spec, key_spec, own_spec, own_spec, tile_spec, tile_spec,
                pl.BlockSpec((1, 1, TILE), lambda h, t, s: (h, 0, t)),
            ],
            out_specs=[tile_spec, key_spec, key_spec, own_spec, own_spec],
            scratch_shapes=[
                pltpu.VMEM((HEAD_DIM, keys), bf16),
                pltpu.VMEM((keys, HEAD_DIM), f32),
                pltpu.VMEM((keys, HEAD_DIM), f32),
            ],
        ),
        out_shape=[
            jax.ShapeDtypeStruct((rows, width), f32),
            jax.ShapeDtypeStruct((keys, width), bf16),
            jax.ShapeDtypeStruct((keys, width), bf16),
            jax.ShapeDtypeStruct((rows - prompt_rows, width), f32),
            jax.ShapeDtypeStruct((rows - prompt_rows, width), f32),
        ],
        compiler_params=pltpu.CompilerParams(
            dimension_semantics=("arbitrary", "arbitrary"), vmem_limit_bytes=56 << 20
        ),
        name="attention_backward",
    )(slab, q, k, v, ko, vo, att, d_att, lse)


def expert_pass(order, order_sets, h, cot, gates, w_gu, w_dn, gu_a, gu_b, dn_a, dn_b):
    shards, parts, rows, part_width = h.shape
    width = parts * part_width
    locals_n = gates.shape[2]
    ff = w_dn.shape[1]
    tiles = rows // TILE
    gu_rank = 2 * RANK

    def body(
        order_ref, set_ref, h_ref, cot_ref, gate_ref, wgu_ref, wdn_ref, gua_ref, gub_ref,
        dna_ref, dnb_ref, y_ref, dh_ref, dgate_ref, ggua_ref, ggub_ref, gdna_ref, gdnb_ref,
        y_acc, dh_acc,
    ):
        step = pl.program_id(0)
        fresh = jnp.logical_or(
            step == 0, set_ref[step] != set_ref[jnp.maximum(step - 1, 0)]
        )

        @pl.when(fresh)
        def _():
            ggua_ref[...] = jnp.zeros_like(ggua_ref)
            ggub_ref[...] = jnp.zeros_like(ggub_ref)
            gdna_ref[...] = jnp.zeros_like(gdna_ref)
            gdnb_ref[...] = jnp.zeros_like(gdnb_ref)

        x = jnp.concatenate([h_ref[0, i] for i in range(parts)], axis=1)
        ct = jnp.concatenate([cot_ref[0, i] for i in range(parts)], axis=1)
        gu_a_rows = gua_ref[0]
        gu_b_rows = gub_ref[0]
        dn_a_rows = dna_ref[0]
        dn_b_rows = dnb_ref[0]
        mid_gu = (ADAPTER_SCALE * dot_nt(x, gu_a_rows)).astype(bf16)
        d_mid_dn = (ADAPTER_SCALE * dot_nt(ct, dn_b_rows)).astype(bf16)
        gu_lane = lax.broadcasted_iota(jnp.int32, mid_gu.shape, 1)
        dn_lane = lax.broadcasted_iota(jnp.int32, d_mid_dn.shape, 1)
        n_all = jnp.zeros(mid_gu.shape, f32)
        mid_dn_all = jnp.zeros(d_mid_dn.shape, f32)
        gate_block = gate_ref[0, 0]
        d_gate_cols = []
        for e in range(locals_n):
            gate_lanes = (gu_lane // RANK) == 2 * e
            up_lanes = (gu_lane // RANK) == 2 * e + 1
            dn_lanes = (dn_lane // RANK) == e
            zero_gu = jnp.zeros_like(mid_gu)
            mid_gate = jnp.where(gate_lanes, mid_gu, zero_gu)
            mid_up = jnp.where(up_lanes, mid_gu, zero_gu)
            d_mid_e = jnp.where(dn_lanes, d_mid_dn, jnp.zeros_like(d_mid_dn))
            g = dot_nn(x, wgu_ref[e, 0]) + dot_nn(mid_gate, gu_b_rows)
            u = dot_nn(x, wgu_ref[e, 1]) + dot_nn(mid_up, gu_b_rows)
            c = dot_nt(ct, wdn_ref[e]) + dot_nn(d_mid_e, dn_a_rows)
            gate = gate_block[:, e : e + 1]
            sig = jax.nn.sigmoid(g)
            silu = g * sig
            hidden = silu * u
            hidden_b = hidden.astype(bf16)
            d_gate_cols.append(jnp.sum(hidden_b.astype(f32) * c, axis=1, keepdims=True))
            d_hidden = gate * c
            d_g = (d_hidden * u * sig * (1.0 + g * (1.0 - sig))).astype(bf16)
            d_u = (d_hidden * silu).astype(bf16)
            gated = (gate * hidden).astype(bf16)
            y_e = dot_nn(gated, wdn_ref[e])
            dh_e = dot_nt(d_g, wgu_ref[e, 0]) + dot_nt(d_u, wgu_ref[e, 1])
            if e == 0:
                y_acc[...] = y_e
                dh_acc[...] = dh_e
            else:
                y_acc[...] += y_e
                dh_acc[...] += dh_e
            mid_dn_all = jnp.where(dn_lanes, dot_nt(gated, dn_a_rows), mid_dn_all)
            n_all = jnp.where(gate_lanes, dot_nt(d_g, gu_b_rows), n_all)
            n_all = jnp.where(up_lanes, dot_nt(d_u, gu_b_rows), n_all)
            ggub_ref[0] += dot_tn(mid_gate, d_g) + dot_tn(mid_up, d_u)
            gdna_ref[0] += dot_tn((gate * d_mid_e.astype(f32)).astype(bf16), hidden_b)
        n_b = (ADAPTER_SCALE * n_all).astype(bf16)
        mid_dn_b = (ADAPTER_SCALE * mid_dn_all).astype(bf16)
        y = (y_acc[...] + dot_nn(mid_dn_b, dn_b_rows)).astype(bf16)
        dh = (dh_acc[...] + dot_nn(n_b, gu_a_rows)).astype(bf16)
        for i in range(parts):
            y_ref[0, i] = y[:, i * part_width : (i + 1) * part_width]
            dh_ref[0, i] = dh[:, i * part_width : (i + 1) * part_width]
        dgate_ref[0, 0] = jnp.concatenate(d_gate_cols, axis=1)
        ggua_ref[0] += dot_tn(n_b, x)
        gdnb_ref[0] += dot_tn(mid_dn_b, ct)

    row_spec = pl.BlockSpec(
        (1, parts, TILE, part_width), lambda i, o, s: (o[i] // tiles, 0, o[i] % tiles, 0)
    )
    gate_spec = pl.BlockSpec(
        (1, 1, TILE, locals_n), lambda i, o, s: (o[i] // tiles, o[i] % tiles, 0, 0)
    )
    gates = gates.reshape(shards, tiles, TILE, locals_n)

    def whole(a):
        zeros = (0,) * a.ndim
        return pl.BlockSpec(a.shape, lambda i, o, s: zeros, pipeline_mode=pl.Buffered(1))

    def of_set(a):
        return pl.BlockSpec((1,) + a.shape[1:], lambda i, o, s: (s[i], 0, 0))

    grads = [jax.ShapeDtypeStruct(a.shape, f32) for a in (gu_a, gu_b, dn_a, dn_b)]
    return pl.pallas_call(
        body,
        grid_spec=pltpu.PrefetchScalarGridSpec(
            num_scalar_prefetch=2,
            grid=(shards * tiles,),
            in_specs=[row_spec, row_spec, gate_spec, whole(w_gu), whole(w_dn)]
            + [of_set(a) for a in (gu_a, gu_b, dn_a, dn_b)],
            out_specs=[row_spec, row_spec, gate_spec] + [of_set(a) for a in grads],
            scratch_shapes=[pltpu.VMEM((TILE, width), f32), pltpu.VMEM((TILE, width), f32)],
        ),
        out_shape=[
            jax.ShapeDtypeStruct(h.shape, bf16),
            jax.ShapeDtypeStruct(h.shape, bf16),
            jax.ShapeDtypeStruct(gates.shape, f32),
        ]
        + grads,
        compiler_params=pltpu.CompilerParams(
            dimension_semantics=("arbitrary",), vmem_limit_bytes=60 << 20
        ),
        name="expert_pass",
    )(order, order_sets, h, cot, gates, w_gu, w_dn, gu_a, gu_b, dn_a, dn_b)


def per_device(
    tokens, cotangent, routes, adapter_ids, norm_in, norm_mid, q_gain, k_gain, w_qkv, w_out,
    w_router, w_gate_up, w_down, qkv_a, qkv_b, out_a, out_b, router_a, router_b, gu_a, gu_b,
    down_a, down_b,
):
    row_count, full_width = tokens.shape
    local_width = q_gain.shape[0]
    local_heads = local_width // HEAD_DIM
    locals_n, ff_local = w_gate_up.shape[0], w_gate_up.shape[3]
    shard_count, slab_count, part_count = (
        lax.axis_size("fsdp"), lax.axis_size("ctx"), lax.axis_size("tp"),
    )
    shard_index, slab_index, part_index = (
        lax.axis_index("fsdp"), lax.axis_index("ctx"), lax.axis_index("tp"),
    )
    part_width = full_width // part_count
    prompt_rows = PROMPT // slab_count
    cont_count = CONTS // slab_count
    tiles, prompt_tiles = row_count // TILE, prompt_rows // TILE
    row_index = jnp.arange(row_count, dtype=jnp.int32)
    tail_offset = jnp.maximum(row_index - prompt_rows, 0)
    leading = row_index < prompt_rows
    positions = jnp.where(
        leading, slab_index * prompt_rows + row_index, PROMPT + tail_offset % CONT_LEN
    )
    cosine, sine_part = angles(positions)
    slab = slab_index.reshape(1).astype(jnp.int32)

    def my_part(x):
        return lax.dynamic_slice_in_dim(x, part_index * part_width, part_width, axis=1)

    def tile_rows(x):
        return x.reshape(tiles, TILE, x.shape[1])

    cont_sets = lax.dynamic_slice_in_dim(adapter_ids[0], 1 + slab_index * cont_count, cont_count)
    tile_sets = jnp.concatenate([jnp.broadcast_to(adapter_ids[0, :1], (prompt_tiles,)), cont_sets])
    all_sets = lax.all_gather(tile_sets, "fsdp", axis=0, tiled=True)
    count_all = all_sets.shape[0]
    tile_at = jnp.arange(count_all, dtype=jnp.int32)
    ahead = (all_sets[None, :] < all_sets[:, None]) | (
        (all_sets[None, :] == all_sets[:, None]) & (tile_at[None, :] < tile_at[:, None])
    )
    rank_of = jnp.sum(ahead.astype(jnp.int32), axis=1)
    at_rank = (rank_of[None, :] == tile_at[:, None]).astype(jnp.int32)
    order = jnp.sum(at_rank * tile_at[None, :], axis=1)
    order_sets = jnp.sum(at_rank * all_sets[None, :], axis=1)
    set_at = jnp.arange(SETS, dtype=jnp.int32)
    present = jnp.any(set_at[:, None] == all_sets[None, :], axis=1)
    tile_hot = (set_at[:, None] == tile_sets[None, :]).astype(f32)

    sets_local = qkv_a.shape[0]

    def as_rows(x):
        return x.reshape(x.shape[0], -1, local_width)

    def router_rows(x):
        flat = x.reshape(x.shape[0], 1, -1)
        return jnp.pad(flat, ((0, 0), (0, 0), (0, local_width - flat.shape[2])))

    pieces = [
        as_rows(qkv_a.transpose(0, 2, 3, 1)),
        as_rows(qkv_b.transpose(0, 2, 1, 3)),
        as_rows(out_a.transpose(0, 2, 1)),
        as_rows(out_b),
        as_rows(router_a.transpose(0, 2, 1)),
        router_rows(router_b),
    ]
    sizes = [p.shape[1] for p in pieces]
    packed = lax.all_gather(jnp.concatenate(pieces, axis=1), "fsdp", axis=0, tiled=True)
    picked = jnp.take(packed, tile_sets, axis=0)
    cuts = [sum(sizes[:i]) for i in range(len(sizes) + 1)]

    def piece(i, shape):
        return picked[:, cuts[i] : cuts[i + 1]].reshape((tiles,) + shape)

    t_qkv_a = piece(0, (3, RANK, full_width))
    t_qkv_b = piece(1, (3, RANK, local_width))
    t_out_a = piece(2, (RANK, local_width))
    t_out_b = piece(3, (RANK, full_width))
    t_router_a = piece(4, (RANK, full_width))
    t_router_b = picked[:, cuts[5], : RANK * EXPERTS].reshape(tiles, RANK, EXPERTS)

    token_vals = tokens.astype(f32)
    cot_vals = cotangent.astype(f32)
    gain_in = norm_in.astype(f32)
    gain_mid = norm_mid.astype(f32)
    gain_q = q_gain.astype(f32)
    gain_k = k_gain.astype(f32)
    first_scale = lax.rsqrt(jnp.mean(token_vals * token_vals, axis=1, keepdims=True) + epsilon)
    h_first = (token_vals * first_scale * gain_in).astype(bf16)
    whole_qkv = lax.all_gather(w_qkv, "fsdp", axis=0, tiled=True)
    proj = jnp.einsum("nd,djo->jno", h_first, whole_qkv, preferred_element_type=f32)
    mid_qkv = (
        ADAPTER_SCALE
        * jnp.einsum("tnd,tjrd->tnjr", tile_rows(h_first), t_qkv_a, preferred_element_type=f32)
    ).astype(bf16)
    proj = proj + jnp.einsum(
        "tnjr,tjro->jtno", mid_qkv, t_qkv_b, preferred_element_type=f32
    ).reshape(3, row_count, local_width)
    q_raw, k_raw = proj[0], proj[1]
    squares = lax.psum(
        jnp.stack([jnp.sum(q_raw * q_raw, axis=1), jnp.sum(k_raw * k_raw, axis=1)]), "tp"
    )
    q_scale = lax.rsqrt(squares[0] / full_width + epsilon)[:, None]
    k_scale = lax.rsqrt(squares[1] / full_width + epsilon)[:, None]

    def heads_of(x):
        return x.reshape(x.shape[0], local_heads, HEAD_DIM)

    query_rows = (
        rotate(heads_of(q_raw * q_scale * gain_q), cosine, sine_part)
        .reshape(row_count, local_width)
        .astype(bf16)
    )
    key_rows = (
        rotate(heads_of(k_raw * k_scale * gain_k), cosine, sine_part)
        .reshape(row_count, local_width)
        .astype(bf16)
    )
    value_rows = proj[2].astype(bf16)
    prompt_keys = lax.all_gather(key_rows[:prompt_rows], "ctx", axis=0, tiled=True)
    prompt_values = lax.all_gather(value_rows[:prompt_rows], "ctx", axis=0, tiled=True)
    key_own, value_own = key_rows[prompt_rows:], value_rows[prompt_rows:]
    attention_rows, log_total = attention_forward(
        slab, query_rows, prompt_keys, prompt_values, key_own, value_own, prompt_rows
    )
    whole_out = lax.all_gather(w_out, "fsdp", axis=1, tiled=True)
    mid_out = (
        ADAPTER_SCALE
        * jnp.einsum("tnd,trd->tnr", tile_rows(attention_rows), t_out_a, preferred_element_type=f32)
    ).astype(bf16)
    branch = lax.psum(
        jnp.dot(attention_rows, whole_out, preferred_element_type=f32)
        + jnp.einsum("tnr,trd->tnd", mid_out, t_out_b, preferred_element_type=f32).reshape(
            row_count, full_width
        ),
        "tp",
    )
    x_mid = token_vals + branch
    mid_scale = lax.rsqrt(jnp.mean(x_mid * x_mid, axis=1, keepdims=True) + epsilon)
    h_second = (x_mid * mid_scale * gain_mid).astype(bf16)
    h_tiles = tile_rows(h_second)
    mid_router = (
        ADAPTER_SCALE
        * jnp.einsum("tnd,trd->tnr", h_tiles, t_router_a, preferred_element_type=f32)
    ).astype(bf16)
    router_logits = jnp.dot(h_second, w_router, preferred_element_type=f32) + jnp.einsum(
        "tnr,tre->tne", mid_router, t_router_b, preferred_element_type=f32
    ).reshape(row_count, EXPERTS)
    expert_probs = jax.nn.softmax(router_logits, axis=1)
    chosen = jnp.any(
        routes[:, :, None] == jnp.arange(EXPERTS, dtype=jnp.int32)[None, None, :], axis=1
    )
    gates = jnp.where(chosen, expert_probs, 0.0)

    def gather_rows(x):
        return lax.all_gather(my_part(x), ("fsdp", "tp"), axis=0, tiled=False).reshape(
            shard_count, part_count, row_count, part_width
        )

    def experts_of_sets(x):
        return lax.all_to_all(x, "fsdp", split_axis=1, concat_axis=0, tiled=True)

    e_gu_a = experts_of_sets(gu_a.transpose(0, 1, 3, 4, 2)).reshape(SETS, -1, full_width)
    e_gu_b = experts_of_sets(gu_b.transpose(0, 1, 3, 2, 4)).reshape(SETS, -1, ff_local)
    e_dn_a = experts_of_sets(down_a.transpose(0, 1, 3, 2)).reshape(SETS, -1, ff_local)
    e_dn_b = experts_of_sets(down_b).reshape(SETS, -1, full_width)
    cot_all = gather_rows(cotangent)
    h_all = gather_rows(h_second)
    gates_all = lax.all_gather(gates, "fsdp", axis=0, tiled=False)
    my_gates = lax.dynamic_slice_in_dim(gates_all, shard_index * locals_n, locals_n, axis=2)
    y_part, dh_part, d_gates_part, g_gu_a, g_gu_b, g_dn_a, g_dn_b = expert_pass(
        order, order_sets, h_all, cot_all, my_gates, w_gate_up.transpose(0, 2, 1, 3), w_down,
        e_gu_a, e_gu_b, e_dn_a, e_dn_b,
    )

    def return_rows(x):
        own = lax.psum_scatter(
            x.reshape(shard_count * part_count, row_count, part_width),
            ("fsdp", "tp"), scatter_dimension=0, tiled=False,
        )
        return own

    d_gates_wide = lax.dynamic_update_slice_in_dim(
        jnp.zeros((shard_count, row_count, EXPERTS), f32),
        d_gates_part.reshape(shard_count, row_count, locals_n),
        shard_index * locals_n, axis=2,
    )
    d_gates = lax.psum(
        lax.psum_scatter(d_gates_wide, "fsdp", scatter_dimension=0, tiled=False), "tp"
    )
    d_second_routed = lax.all_gather(return_rows(dh_part), "tp", axis=1, tiled=True).astype(f32)
    mixed = lax.all_gather(
        (my_part(x_mid) + return_rows(y_part).astype(f32)).astype(bf16), "tp", axis=1, tiled=True
    )

    d_probs = jnp.where(chosen, d_gates, 0.0)
    d_logits = (
        expert_probs * (d_probs - jnp.sum(expert_probs * d_probs, axis=1, keepdims=True))
    ).astype(bf16)
    dl_tiles = tile_rows(d_logits)
    d_mid_router = (
        ADAPTER_SCALE
        * jnp.einsum("tne,tre->tnr", dl_tiles, t_router_b, preferred_element_type=f32)
    ).astype(bf16)
    g_router_b = jnp.einsum("tnr,tne->tre", mid_router, dl_tiles, preferred_element_type=f32)
    g_router_a = jnp.einsum("tnr,tnd->trd", d_mid_router, h_tiles, preferred_element_type=f32)
    d_second = (
        d_second_routed
        + jnp.einsum("ne,de->nd", d_logits, w_router, preferred_element_type=f32)
        + jnp.einsum("tnr,trd->tnd", d_mid_router, t_router_a, preferred_element_type=f32).reshape(
            row_count, full_width
        )
    )
    d_x_mid = cot_vals + rms_back(x_mid, gain_mid, d_second, mid_scale, full_width)
    d_branch = d_x_mid.astype(bf16)
    db_tiles = tile_rows(d_branch)
    d_mid_out = (
        ADAPTER_SCALE
        * jnp.einsum("tnd,trd->tnr", db_tiles, t_out_b, preferred_element_type=f32)
    ).astype(bf16)
    d_att = jnp.einsum("nc,oc->no", d_branch, whole_out, preferred_element_type=f32) + jnp.einsum(
        "tnr,tro->tno", d_mid_out, t_out_a, preferred_element_type=f32
    ).reshape(row_count, local_width)
    g_out_b = jnp.einsum("tnr,tnd->trd", mid_out, db_tiles, preferred_element_type=f32)
    g_out_a = jnp.einsum(
        "tnr,tno->tro", d_mid_out, tile_rows(attention_rows), preferred_element_type=f32
    )
    d_att_rows = d_att.astype(bf16)
    d_query, d_key_all, d_value_all, d_key_own, d_value_own = attention_backward(
        slab, query_rows, prompt_keys, prompt_values, key_own, value_own, attention_rows,
        d_att_rows, log_total, prompt_rows,
    )
    d_key_prompt = lax.psum_scatter(d_key_all, "ctx", scatter_dimension=0, tiled=True)
    d_value_prompt = lax.psum_scatter(d_value_all, "ctx", scatter_dimension=0, tiled=True)
    d_key = jnp.concatenate([d_key_prompt.astype(f32), d_key_own], axis=0)
    d_value = jnp.concatenate([d_value_prompt.astype(f32), d_value_own], axis=0)
    d_q_norm = rotate(heads_of(d_query), cosine, -sine_part).reshape(row_count, local_width)
    d_k_norm = rotate(heads_of(d_key), cosine, -sine_part).reshape(row_count, local_width)
    dots = lax.psum(
        jnp.stack(
            [jnp.sum(gain_q * q_raw * d_q_norm, axis=1), jnp.sum(gain_k * k_raw * d_k_norm, axis=1)]
        ),
        "tp",
    )
    d_q_raw = (
        q_scale * gain_q * d_q_norm
        - q_raw * (q_scale * q_scale * q_scale) * dots[0][:, None] / full_width
    )
    d_k_raw = (
        k_scale * gain_k * d_k_norm
        - k_raw * (k_scale * k_scale * k_scale) * dots[1][:, None] / full_width
    )
    d_proj = jnp.stack([d_q_raw, d_k_raw, d_value], axis=0).astype(bf16)
    dp_tiles = d_proj.reshape(3, tiles, TILE, local_width)
    d_mid_qkv = (
        ADAPTER_SCALE
        * jnp.einsum("jtno,tjro->tnjr", dp_tiles, t_qkv_b, preferred_element_type=f32)
    ).astype(bf16)
    d_first = lax.psum(
        jnp.einsum("jno,djo->nd", d_proj, whole_qkv, preferred_element_type=f32)
        + jnp.einsum("tnjr,tjrd->tnd", d_mid_qkv, t_qkv_a, preferred_element_type=f32).reshape(
            row_count, full_width
        ),
        "tp",
    )
    grad_input = d_x_mid + rms_back(token_vals, gain_in, d_first, first_scale, full_width)
    g_qkv_b = jnp.einsum("tnjr,jtno->tjro", mid_qkv, dp_tiles, preferred_element_type=f32)
    g_qkv_a = jnp.einsum(
        "tnjr,tnd->tjrd", d_mid_qkv, tile_rows(h_first), preferred_element_type=f32
    )

    def to_sets(pieces_):
        rows_ = jnp.concatenate(pieces_, axis=1)
        return jnp.sum(tile_hot[:, :, None, None] * rows_[None], axis=1).astype(bf16)

    def reduced(x, axes):
        mine = lax.psum_scatter(x, "fsdp", scatter_dimension=0, tiled=True)
        return lax.psum(mine, axes).astype(f32)

    both = reduced(to_sets([as_rows(g_qkv_a), as_rows(g_out_b)]), ("ctx", "tp"))
    one = reduced(
        to_sets(
            [as_rows(g_qkv_b), as_rows(g_out_a), as_rows(g_router_a), router_rows(g_router_b)]
        ),
        "ctx",
    )
    n0, n1, n2, n3, n4 = sizes[0], sizes[1], sizes[2], sizes[3], sizes[4]
    grad_qkv_a = both[:, :n0].reshape(sets_local, 3, RANK, full_width).transpose(0, 3, 1, 2)
    grad_out_b = both[:, n0 : n0 + n3].reshape(out_b.shape)
    grad_qkv_b = one[:, :n1].reshape(sets_local, 3, RANK, local_width).transpose(0, 2, 1, 3)
    grad_out_a = one[:, n1 : n1 + n2].reshape(sets_local, RANK, local_width).transpose(0, 2, 1)
    grad_router_a = (
        one[:, n1 + n2 : n1 + n2 + n4].reshape(sets_local, RANK, full_width).transpose(0, 2, 1)
    )
    grad_router_b = one[:, n1 + n2 + n4, : RANK * EXPERTS].reshape(router_b.shape)

    def expert_grad(g, axes):
        g = jnp.where(present[:, None, None], g, 0.0).astype(bf16)
        g = lax.psum(g, axes)
        g = g.reshape(SETS, locals_n, -1, g.shape[2])
        return lax.all_to_all(g, "fsdp", split_axis=0, concat_axis=1, tiled=True).astype(f32)

    grad_gu_a = (
        expert_grad(g_gu_a, ("ctx", "tp"))
        .reshape(sets_local, EXPERTS, 2, RANK, full_width)
        .transpose(0, 1, 4, 2, 3)
    )
    grad_gu_b = (
        expert_grad(g_gu_b, "ctx")
        .reshape(sets_local, EXPERTS, 2, RANK, ff_local)
        .transpose(0, 1, 3, 2, 4)
    )
    grad_down_a = expert_grad(g_dn_a, "ctx").transpose(0, 1, 3, 2)
    grad_down_b = expert_grad(g_dn_b, ("ctx", "tp"))
    return (
        mixed, grad_input, grad_qkv_a, grad_qkv_b, grad_out_a, grad_out_b, grad_router_a,
        grad_router_b, grad_gu_a, grad_gu_b, grad_down_a, grad_down_b,
    )


def solution(mesh):
    return jax.shard_map(
        per_device,
        mesh=mesh,
        in_specs=(
            P(("fsdp", "ctx"), None),
            P(("fsdp", "ctx"), None),
            P(("fsdp", "ctx"), None),
            P("fsdp", None),
            P(),
            P(),
            P("tp"),
            P("tp"),
            P("fsdp", None, "tp"),
            P("tp", "fsdp"),
            P(),
            P("fsdp", None, None, "tp"),
            P("fsdp", "tp", None),
            P("fsdp", None, None, None),
            P("fsdp", None, None, "tp"),
            P("fsdp", "tp", None),
            P("fsdp", None, None),
            P("fsdp", None, None),
            P("fsdp", None, None),
            P("fsdp", None, None, None, None),
            P("fsdp", None, None, None, "tp"),
            P("fsdp", None, "tp", None),
            P("fsdp", None, None, None),
        ),
        out_specs=(
            P(("fsdp", "ctx"), None),
            P(("fsdp", "ctx"), None),
            P("fsdp", None, None, None),
            P("fsdp", None, None, "tp"),
            P("fsdp", "tp", None),
            P("fsdp", None, None),
            P("fsdp", None, None),
            P("fsdp", None, None),
            P("fsdp", None, None, None, None),
            P("fsdp", None, None, None, "tp"),
            P("fsdp", None, "tp", None),
            P("fsdp", None, None, None),
        ),
        check_vma=False,
    )
```

```python
import jax
import jax.numpy as jnp
from jax import lax
from jax.experimental import pallas as pl
from jax.experimental.pallas import tpu as pltpu
from jax.sharding import PartitionSpec as P

HEAD_DIM = 128
TOPK = 8
EXPERTS = 16
RANK = 16
PROMPT = 2048
CONT_LEN = 256
CONTS = 8
SETS = 8

epsilon = 1e-05
ADAPTER_SCALE = 0.5
ROPE_BASE = 10000.0
masked_score = -1e30
TILE = CONT_LEN
SCORE_SCALE = HEAD_DIM ** (-0.5)
f32 = jnp.float32
bf16 = jnp.bfloat16


def dot_nn(a, b):
    return lax.dot_general(a, b, (((1,), (0,)), ((), ())), preferred_element_type=f32)


def dot_nt(a, b):
    return lax.dot_general(a, b, (((1,), (1,)), ((), ())), preferred_element_type=f32)


def dot_tn(a, b):
    return lax.dot_general(a, b, (((0,), (0,)), ((), ())), preferred_element_type=f32)


def rms_back(value, gain, grad, scale_col, full_width):
    inner = jnp.sum(gain * value * grad, axis=-1, keepdims=True)
    return (
        scale_col * gain * grad - value * (scale_col * scale_col * scale_col) * inner / full_width
    )


def angles(positions):
    freqs = ROPE_BASE ** (-(2.0 * jnp.arange(HEAD_DIM // 2, dtype=f32)) / HEAD_DIM)
    turned = positions.astype(f32)[:, None] * freqs[None, :]
    return (jnp.cos(turned)[:, None, :], jnp.sin(turned)[:, None, :])


def rotate(value, cosine, sine_part):
    half_dim = value.shape[-1] // 2
    first_half = value[..., :half_dim]
    second_half = value[..., half_dim:]
    return jnp.concatenate(
        [
            first_half * cosine - second_half * sine_part,
            second_half * cosine + first_half * sine_part,
        ],
        axis=-1,
    )


def attention_scores(k_ref, q, slab_ref, tile, prompt_rows, is_prompt):
    scores = dot_nt(k_ref[...], q) * SCORE_SCALE
    if not is_prompt:
        return scores
    block_at = lax.broadcasted_iota(jnp.int32, (prompt_rows, scores.shape[1]), 0)
    key_at = jnp.concatenate(
        [
            block_at + jnp.bitwise_xor(slab_ref[0], b) * prompt_rows
            for b in range(scores.shape[0] // prompt_rows)
        ],
        axis=0,
    )
    query_at = (
        slab_ref[0] * prompt_rows + tile * TILE + lax.broadcasted_iota(jnp.int32, scores.shape, 1)
    )
    return jnp.where(key_at <= query_at, scores, masked_score)


def own_scores(ko_ref, q):
    scores = dot_nt(ko_ref[...], q) * SCORE_SCALE
    key_at = lax.broadcasted_iota(jnp.int32, scores.shape, 0)
    query_at = lax.broadcasted_iota(jnp.int32, scores.shape, 1)
    return jnp.where(key_at <= query_at, scores, masked_score)


def attention_forward(slab, q, k, v, ko, vo, prompt_rows):
    rows, width = q.shape
    heads, tiles, prompt_tiles = width // HEAD_DIM, rows // TILE, prompt_rows // TILE
    keys = k.shape[0]

    def body(slab_ref, q_ref, k_ref, v_ref, ko_ref, vo_ref, att_ref, lse_ref, vt_ref):
        tile = pl.program_id(1)

        @pl.when(tile == 0)
        def _():
            vt_ref[...] = v_ref[...].T

        query = q_ref[...]

        def finish(total, peak, out_t):
            att_ref[...] = (out_t / total).T.astype(bf16)
            lse_ref[0] = peak + jnp.log(total)

        @pl.when(tile < prompt_tiles)
        def _():
            scores = attention_scores(k_ref, query, slab_ref, tile, prompt_rows, True)
            peak = jnp.max(scores, axis=0, keepdims=True)
            probs = jnp.exp(scores - peak)
            total = jnp.sum(probs, axis=0, keepdims=True)
            finish(total, peak, dot_nn(vt_ref[...], probs.astype(bf16)))

        @pl.when(tile >= prompt_tiles)
        def _():
            scores = attention_scores(k_ref, query, slab_ref, tile, prompt_rows, False)
            own = own_scores(ko_ref, query)
            peak = jnp.maximum(
                jnp.max(scores, axis=0, keepdims=True), jnp.max(own, axis=0, keepdims=True)
            )
            probs = jnp.exp(scores - peak)
            own_probs = jnp.exp(own - peak)
            total = jnp.sum(probs, axis=0, keepdims=True) + jnp.sum(
                own_probs, axis=0, keepdims=True
            )
            out_t = dot_nn(vt_ref[...], probs.astype(bf16)) + dot_nn(
                vo_ref[...].T, own_probs.astype(bf16)
            )
            finish(total, peak, out_t)

    tile_spec = pl.BlockSpec((TILE, HEAD_DIM), lambda h, t, s: (t, h))
    key_spec = pl.BlockSpec((keys, HEAD_DIM), lambda h, t, s: (0, h))
    own_spec = pl.BlockSpec(
        (TILE, HEAD_DIM), lambda h, t, s: (jnp.maximum(t - prompt_tiles, 0), h)
    )
    return pl.pallas_call(
        body,
        grid_spec=pltpu.PrefetchScalarGridSpec(
            num_scalar_prefetch=1,
            grid=(heads, tiles),
            in_specs=[tile_spec, key_spec, key_spec, own_spec, own_spec],
            out_specs=[tile_spec, pl.BlockSpec((1, 1, TILE), lambda h, t, s: (h, 0, t))],
            scratch_shapes=[pltpu.VMEM((HEAD_DIM, keys), bf16)],
        ),
        out_shape=[
            jax.ShapeDtypeStruct((rows, width), bf16),
            jax.ShapeDtypeStruct((heads, 1, rows), f32),
        ],
        compiler_params=pltpu.CompilerParams(
            dimension_semantics=("arbitrary", "arbitrary"), vmem_limit_bytes=56 << 20
        ),
        name="attention_forward",
    )(slab, q, k, v, ko, vo)


def attention_backward(slab, q, k, v, ko, vo, att, d_att, lse, prompt_rows):
    rows, width = q.shape
    heads, tiles, prompt_tiles = width // HEAD_DIM, rows // TILE, prompt_rows // TILE
    keys = k.shape[0]

    def body(
        slab_ref, q_ref, k_ref, v_ref, ko_ref, vo_ref, att_ref, da_ref, lse_ref,
        dq_ref, dk_ref, dv_ref, dko_ref, dvo_ref, kt_ref, dka_ref, dva_ref,
    ):
        tile = pl.program_id(1)

        @pl.when(tile == 0)
        def _():
            kt_ref[...] = k_ref[...].T
            dka_ref[...] = jnp.zeros_like(dka_ref)
            dva_ref[...] = jnp.zeros_like(dva_ref)

        query = q_ref[...]
        d_out = da_ref[...]
        delta = jnp.sum(
            (d_out.astype(f32) * att_ref[...].astype(f32)).T, axis=0, keepdims=True
        )
        log_total = lse_ref[0]

        def prompt_keys(is_prompt):
            scores = attention_scores(k_ref, query, slab_ref, tile, prompt_rows, is_prompt)
            probs = jnp.exp(scores - log_total)
            d_probs = dot_nt(v_ref[...], d_out)
            d_scores = (probs * (d_probs - delta)).astype(bf16)
            dka_ref[...] += dot_nn(d_scores, query)
            dva_ref[...] += dot_nn(probs.astype(bf16), d_out)
            return dot_nn(kt_ref[...], d_scores)

        @pl.when(tile < prompt_tiles)
        def _():
            dq_ref[...] = prompt_keys(True).T * SCORE_SCALE

        @pl.when(tile >= prompt_tiles)
        def _():
            dq_t = prompt_keys(False)
            probs = jnp.exp(own_scores(ko_ref, query) - log_total)
            d_probs = dot_nt(vo_ref[...], d_out)
            d_scores = (probs * (d_probs - delta)).astype(bf16)
            dko_ref[...] = dot_nn(d_scores, query) * SCORE_SCALE
            dvo_ref[...] = dot_nn(probs.astype(bf16), d_out)
            dq_ref[...] = (dq_t + dot_nn(ko_ref[...].T, d_scores)).T * SCORE_SCALE

        @pl.when(tile == tiles - 1)
        def _():
            dk_ref[...] = (dka_ref[...] * SCORE_SCALE).astype(bf16)
            dv_ref[...] = dva_ref[...].astype(bf16)

    tile_spec = pl.BlockSpec((TILE, HEAD_DIM), lambda h, t, s: (t, h))
    key_spec = pl.BlockSpec((keys, HEAD_DIM), lambda h, t, s: (0, h))
    own_spec = pl.BlockSpec(
        (TILE, HEAD_DIM), lambda h, t, s: (jnp.maximum(t - prompt_tiles, 0), h)
    )
    return pl.pallas_call(
        body,
        grid_spec=pltpu.PrefetchScalarGridSpec(
            num_scalar_prefetch=1,
            grid=(heads, tiles),
            in_specs=[
                tile_spec, key_spec, key_spec, own_spec, own_spec, tile_spec, tile_spec,
                pl.BlockSpec((1, 1, TILE), lambda h, t, s: (h, 0, t)),
            ],
            out_specs=[tile_spec, key_spec, key_spec, own_spec, own_spec],
            scratch_shapes=[
                pltpu.VMEM((HEAD_DIM, keys), bf16),
                pltpu.VMEM((keys, HEAD_DIM), f32),
                pltpu.VMEM((keys, HEAD_DIM), f32),
            ],
        ),
        out_shape=[
            jax.ShapeDtypeStruct((rows, width), f32),
            jax.ShapeDtypeStruct((keys, width), bf16),
            jax.ShapeDtypeStruct((keys, width), bf16),
            jax.ShapeDtypeStruct((rows - prompt_rows, width), f32),
            jax.ShapeDtypeStruct((rows - prompt_rows, width), f32),
        ],
        compiler_params=pltpu.CompilerParams(
            dimension_semantics=("arbitrary", "arbitrary"), vmem_limit_bytes=56 << 20
        ),
        name="attention_backward",
    )(slab, q, k, v, ko, vo, att, d_att, lse)


def expert_pass(order, order_sets, part, h, cot, gates, w_gu, w_dn, adapters, sums):
    halved = isinstance(h, tuple)
    rows = h[0].shape[0] if halved else h.shape[0]
    width = w_gu.shape[2]
    part_width = width // 2
    locals_n = gates.shape[1]
    tiles = rows // TILE

    def body(
        order_ref, set_ref, part_ref, h0_ref, h1_ref, cot0_ref, cot1_ref, gate_ref, wgu_ref,
        wdn_ref, wide_ref, slim_ref, swide_ref, sslim_ref,
        yk_ref, ys_ref, dhk_ref, dhs_ref, dgate_ref, gwide_ref, gslim_ref,
        y_acc, dh_acc, x_ref, ct_ref, n_ref, mid_ref,
    ):
        step = pl.program_id(0)
        fresh = jnp.logical_or(
            step == 0, set_ref[step] != set_ref[jnp.maximum(step - 1, 0)]
        )

        @pl.when(fresh)
        def _():
            gwide_ref[...] = swide_ref[...]
            gslim_ref[...] = sslim_ref[...]

        low_first = part_ref[0] == 0

        def join(first, second):
            x_ref[:, :part_width] = h0_ref[...] if first else h1_ref[...]
            x_ref[:, part_width:] = h1_ref[...] if first else h0_ref[...]
            ct_ref[:, :part_width] = cot0_ref[...] if first else cot1_ref[...]
            ct_ref[:, part_width:] = cot1_ref[...] if first else cot0_ref[...]

        if halved:
            pl.when(low_first)(lambda: join(True, False))
            pl.when(jnp.logical_not(low_first))(lambda: join(False, True))
        else:
            join(True, False)
        x = x_ref[...]
        ct = ct_ref[...]
        wide = wide_ref[0]
        slim = slim_ref[0]
        lane = lax.broadcasted_iota(jnp.int32, (TILE, wide.shape[0]), 1)
        mid_gu = (ADAPTER_SCALE * dot_nt(x, wide)).astype(bf16)
        d_mid_dn = (ADAPTER_SCALE * dot_nt(ct, wide)).astype(bf16)
        zero_mid = jnp.zeros_like(mid_gu)
        n_ref[...] = jnp.zeros_like(n_ref)
        mid_ref[...] = jnp.zeros_like(mid_ref)
        y_acc[...] = jnp.zeros_like(y_acc)
        dh_acc[...] = jnp.zeros_like(dh_acc)
        gate_block = gate_ref[...]
        gate_lane = lax.broadcasted_iota(jnp.int32, gate_block.shape, 1)

        def expert(e, d_gates):
            gate_lanes = (lane // RANK) == 3 * e
            up_lanes = (lane // RANK) == 3 * e + 1
            dn_lanes = (lane // RANK) == 3 * e + 2
            mid_gate = jnp.where(gate_lanes, mid_gu, zero_mid)
            mid_up = jnp.where(up_lanes, mid_gu, zero_mid)
            d_mid_e = jnp.where(dn_lanes, d_mid_dn, zero_mid)
            g = dot_nn(x_ref[...], wgu_ref[e, 0]) + dot_nn(mid_gate, slim)
            u = dot_nn(x_ref[...], wgu_ref[e, 1]) + dot_nn(mid_up, slim)
            c = dot_nt(ct_ref[...], wdn_ref[e]) + dot_nn(d_mid_e, slim)
            gate = jnp.sum(jnp.where(gate_lane == e, gate_block, 0.0), axis=1, keepdims=True)
            sig = jax.nn.sigmoid(g)
            silu = g * sig
            hidden = silu * u
            hidden_b = hidden.astype(bf16)
            d_gate = jnp.sum(hidden_b.astype(f32) * c, axis=1, keepdims=True)
            d_hidden = gate * c
            d_g = (d_hidden * u * sig * (1.0 + g * (1.0 - sig))).astype(bf16)
            d_u = (d_hidden * silu).astype(bf16)
            gated = (gate * hidden).astype(bf16)
            y_acc[...] += dot_nn(gated, wdn_ref[e])
            dh_acc[...] += dot_nt(d_g, wgu_ref[e, 0]) + dot_nt(d_u, wgu_ref[e, 1])
            mid_ref[...] = jnp.where(dn_lanes, dot_nt(gated, slim), mid_ref[...])
            n_e = jnp.where(gate_lanes, dot_nt(d_g, slim), n_ref[...])
            n_ref[...] = jnp.where(up_lanes, dot_nt(d_u, slim), n_e)
            gslim_ref[0] += (
                dot_tn(mid_gate, d_g)
                + dot_tn(mid_up, d_u)
                + dot_tn((gate * d_mid_e.astype(f32)).astype(bf16), hidden_b)
            )
            return jnp.where(gate_lane == e, d_gate, d_gates)

        dgate_ref[...] = lax.fori_loop(0, locals_n, expert, jnp.zeros(gate_block.shape, f32))
        n_b = (ADAPTER_SCALE * n_ref[...]).astype(bf16)
        mid_dn_b = (ADAPTER_SCALE * mid_ref[...]).astype(bf16)
        y = (y_acc[...] + dot_nn(mid_dn_b, wide)).astype(bf16)
        dh = (dh_acc[...] + dot_nn(n_b, wide)).astype(bf16)

        def part_out(keep_low):
            low, high = slice(0, part_width), slice(part_width, width)
            keep, send = (low, high) if keep_low else (high, low)
            yk_ref[...] = y[:, keep]
            ys_ref[...] = y[:, send]
            dhk_ref[...] = dh[:, keep]
            dhs_ref[...] = dh[:, send]

        pl.when(low_first)(lambda: part_out(True))
        pl.when(jnp.logical_not(low_first))(lambda: part_out(False))
        gwide_ref[0] += dot_tn(n_b, x) + dot_tn(mid_dn_b, ct)

    def row_spec(column):
        return pl.BlockSpec((TILE, part_width), lambda i, o, s, p: (o[i], column))

    gate_spec = pl.BlockSpec((TILE, locals_n), lambda i, o, s, p: (o[i], 0))

    def whole(a):
        zeros = (0,) * a.ndim
        return pl.BlockSpec(a.shape, lambda i, o, s, p: zeros, pipeline_mode=pl.Buffered(1))

    def of_set(a):
        return pl.BlockSpec((1,) + a.shape[1:], lambda i, o, s, p: (s[i], 0, 0))

    if halved:
        row_args = h + cot
        row_specs = [row_spec(0)] * 4
    else:
        row_args = (h, h, cot, cot)
        row_specs = [row_spec(0), row_spec(1)] * 2
    half = jax.ShapeDtypeStruct((rows, part_width), bf16)
    return pl.pallas_call(
        body,
        grid_spec=pltpu.PrefetchScalarGridSpec(
            num_scalar_prefetch=3,
            grid=(tiles,),
            in_specs=row_specs + [gate_spec, whole(w_gu), whole(w_dn)]
            + [of_set(a) for a in adapters] + [of_set(a) for a in sums],
            out_specs=[row_spec(0)] * 4 + [gate_spec] + [of_set(a) for a in sums],
            scratch_shapes=[
                pltpu.VMEM((TILE, width), f32), pltpu.VMEM((TILE, width), f32),
                pltpu.VMEM((TILE, width), bf16), pltpu.VMEM((TILE, width), bf16),
                pltpu.VMEM((TILE, adapters[0].shape[1]), f32),
                pltpu.VMEM((TILE, adapters[0].shape[1]), f32),
            ],
        ),
        out_shape=[half] * 4 + [jax.ShapeDtypeStruct(gates.shape, f32)]
        + [jax.ShapeDtypeStruct(a.shape, f32) for a in sums],
        input_output_aliases={12 + i: 5 + i for i in range(2)},
        compiler_params=pltpu.CompilerParams(
            dimension_semantics=("arbitrary",), vmem_limit_bytes=60 << 20
        ),
        name="expert_pass",
    )(order, order_sets, part, *row_args, gates, w_gu, w_dn, *adapters, *sums)


def per_device(
    tokens, cotangent, routes, adapter_ids, norm_in, norm_mid, q_gain, k_gain, w_qkv, w_out,
    w_router, w_gate_up, w_down, qkv_a, qkv_b, out_a, out_b, router_a, router_b, gu_a, gu_b,
    down_a, down_b,
):
    row_count, full_width = tokens.shape
    local_width = q_gain.shape[0]
    local_heads = local_width // HEAD_DIM
    locals_n, ff_local = w_gate_up.shape[0], w_gate_up.shape[3]
    shard_count, slab_count, part_count = (
        lax.axis_size("fsdp"), lax.axis_size("ctx"), lax.axis_size("tp"),
    )
    shard_index, slab_index, part_index = (
        lax.axis_index("fsdp"), lax.axis_index("ctx"), lax.axis_index("tp"),
    )
    part_width = full_width // part_count
    prompt_rows = PROMPT // slab_count
    cont_count = CONTS // slab_count
    tiles, prompt_tiles = row_count // TILE, prompt_rows // TILE
    row_index = jnp.arange(row_count, dtype=jnp.int32)
    tail_offset = jnp.maximum(row_index - prompt_rows, 0)
    leading = row_index < prompt_rows
    positions = jnp.where(
        leading, slab_index * prompt_rows + row_index, PROMPT + tail_offset % CONT_LEN
    )
    cosine, sine_part = angles(positions)
    slab = slab_index.reshape(1).astype(jnp.int32)

    def my_part(x):
        return lax.dynamic_slice_in_dim(x, part_index * part_width, part_width, axis=1)

    def tile_rows(x):
        return x.reshape(tiles, TILE, x.shape[1])

    def from_shard(x, s):
        return lax.ppermute(
            x, "fsdp", [(i, (i - s) % shard_count) for i in range(shard_count)]
        )

    def to_shard(x, s):
        return lax.ppermute(
            x, "fsdp", [(i, (i + s) % shard_count) for i in range(shard_count)]
        )

    def swap(x):
        return lax.ppermute(x, "tp", [(0, 1), (1, 0)])

    def across(x, bit):
        return lax.ppermute(x, "ctx", [(i, i ^ bit) for i in range(slab_count)])

    def sum_parts(x):
        return x + swap(x)

    def join_parts(mine, other):
        low_first = part_index == 0
        return jnp.concatenate(
            [jnp.where(low_first, mine, other), jnp.where(low_first, other, mine)], axis=1
        )

    def my_slab(x, axis):
        size = x.shape[axis] // slab_count
        return lax.dynamic_slice_in_dim(x, slab_index * size, size, axis=axis)

    def by_shard(pieces_, index):
        return jnp.take(jnp.stack(pieces_), index % shard_count, axis=0)

    shard_at = jnp.arange(shard_count, dtype=jnp.int32)
    slab_bits = [1 << i for i in range(slab_count.bit_length() - 1)]

    cont_sets = lax.dynamic_slice_in_dim(adapter_ids[0], 1 + slab_index * cont_count, cont_count)
    tile_sets = jnp.concatenate([jnp.broadcast_to(adapter_ids[0, :1], (prompt_tiles,)), cont_sets])
    step_sets = jnp.stack([tile_sets] + [from_shard(tile_sets, s) for s in range(1, shard_count)])
    sets_local = qkv_a.shape[0]
    step_sets = (
        (step_sets // sets_local - shard_index) % shard_count * sets_local + step_sets % sets_local
    )
    tile_at = jnp.arange(tiles, dtype=jnp.int32)
    left, right = step_sets[:, None, :], step_sets[:, :, None]
    ahead = (left < right) | ((left == right) & (tile_at[None, None, :] < tile_at[None, :, None]))
    rank_of = jnp.sum(ahead.astype(jnp.int32), axis=2)
    at_rank = (rank_of[:, None, :] == tile_at[None, :, None]).astype(jnp.int32)
    step_order = jnp.sum(at_rank * tile_at[None, None, :], axis=2)
    step_order_sets = jnp.sum(at_rank * left, axis=2)
    set_at = jnp.arange(SETS, dtype=jnp.int32)
    tile_hot = (set_at[:, None] == tile_sets[None, :]).astype(f32)


    def as_rows(x):
        return x.reshape(x.shape[0], -1, local_width)

    def router_rows(x):
        flat = x.reshape(x.shape[0], 1, -1)
        return jnp.pad(flat, ((0, 0), (0, 0), (0, local_width - flat.shape[2])))

    pieces = [
        as_rows(qkv_a.transpose(0, 2, 3, 1)),
        as_rows(qkv_b.transpose(0, 2, 1, 3)),
        as_rows(out_a.transpose(0, 2, 1)),
        as_rows(out_b),
        as_rows(router_a.transpose(0, 2, 1)),
        router_rows(router_b),
    ]
    sizes = [p.shape[1] for p in pieces]
    rows_n = sum(sizes)
    rows_pad = -rows_n % (16 * slab_count)
    packed = my_slab(
        jnp.pad(jnp.concatenate(pieces, axis=1), ((0, 0), (0, rows_pad), (0, 0))), 1
    )
    packed = lax.all_gather(packed, ("fsdp", "ctx"), axis=0, tiled=False)
    packed = packed.reshape((shard_count, slab_count) + packed.shape[1:]).transpose(0, 2, 1, 3, 4)
    packed = packed.reshape(SETS, rows_n + rows_pad, local_width)
    picked = jnp.take(packed, tile_sets, axis=0)
    cuts = [sum(sizes[:i]) for i in range(len(sizes) + 1)]

    def piece(i, shape):
        return picked[:, cuts[i] : cuts[i + 1]].reshape((tiles,) + shape)

    t_qkv_a = piece(0, (3, RANK, full_width))
    t_qkv_b = piece(1, (3, RANK, local_width))
    t_out_a = piece(2, (RANK, local_width))
    t_out_b = piece(3, (RANK, full_width))
    t_router_a = piece(4, (RANK, full_width))
    t_router_b = picked[:, cuts[5], : RANK * EXPERTS].reshape(tiles, RANK, EXPERTS)

    token_vals = tokens.astype(f32)
    cot_vals = cotangent.astype(f32)
    gain_in = norm_in.astype(f32)
    gain_mid = norm_mid.astype(f32)
    gain_q = q_gain.astype(f32)
    gain_k = k_gain.astype(f32)
    first_scale = lax.rsqrt(jnp.mean(token_vals * token_vals, axis=1, keepdims=True) + epsilon)
    h_first = (token_vals * first_scale * gain_in).astype(bf16)

    def exchange(x, bits):
        blocks = {0: x}
        for bit in bits:
            names = sorted(blocks)
            got = across(jnp.stack([blocks[i] for i in names]), bit)
            blocks.update({i ^ bit: got[at] for at, i in enumerate(names)})
        return [blocks[i] for i in range(slab_count)]

    half_n = shard_count // 2
    near_at = jnp.bitwise_xor(jnp.arange(slab_count, dtype=jnp.int32), slab_index)[None, :]
    step_at = ((shard_at - shard_index) % shard_count)[:, None]
    row_at = (step_at // half_n) * (half_n * slab_count) + near_at * half_n + step_at % half_n
    row_at = row_at.reshape(-1)

    def fetch(x):
        mine = my_slab(x, 0)
        return [mine] + [from_shard(mine, s) for s in range(1, shard_count)]

    def spread(got):
        near = exchange(jnp.stack(got[:half_n]), slab_bits)
        far = exchange(jnp.stack(got[half_n:]), slab_bits[::-1])
        rows_ = jnp.concatenate(near + far, axis=0)
        return jnp.take(rows_, row_at, axis=0).reshape(full_width, local_width)

    got_k = fetch(w_qkv[:, 1])
    got_k, w_v, w_q = lax.optimization_barrier((got_k, w_qkv[:, 2], w_qkv[:, 0]))
    got_v = fetch(w_v)
    got_v, w_q = lax.optimization_barrier((got_v, w_q))
    got_q = fetch(w_q)
    got_q, w_out, cot_mine, gu_a, gu_b, down_a, down_b = lax.optimization_barrier(
        (got_q, w_out, my_part(cotangent), gu_a, gu_b, down_a, down_b)
    )
    weights = [spread(got_q), spread(got_k), spread(got_v)]
    mid_qkv = (
        ADAPTER_SCALE
        * jnp.einsum("tnd,tjrd->tnjr", tile_rows(h_first), t_qkv_a, preferred_element_type=f32)
    ).astype(bf16)

    def project(j):
        return jnp.dot(h_first, weights[j], preferred_element_type=f32) + jnp.einsum(
            "tnr,tro->tno", mid_qkv[:, :, j], t_qkv_b[:, j], preferred_element_type=f32
        ).reshape(row_count, local_width)

    def scale_of(raw):
        squares = sum_parts(jnp.sum(raw * raw, axis=1))
        return lax.rsqrt(squares / full_width + epsilon)[:, None]

    k_raw = project(1)
    k_scale = scale_of(k_raw)
    value_rows = project(2).astype(bf16)
    q_raw = project(0)
    q_scale = scale_of(q_raw)

    def heads_of(x):
        return x.reshape(x.shape[0], local_heads, HEAD_DIM)

    query_rows = (
        rotate(heads_of(q_raw * q_scale * gain_q), cosine, sine_part)
        .reshape(row_count, local_width)
        .astype(bf16)
    )
    key_rows = (
        rotate(heads_of(k_raw * k_scale * gain_k), cosine, sine_part)
        .reshape(row_count, local_width)
        .astype(bf16)
    )

    def exchange_back(x, bits):
        blocks = {i: x[i * prompt_rows : (i + 1) * prompt_rows] for i in range(slab_count)}
        for bit in bits:
            sent = sorted(i for i in blocks if i & bit)
            got = across(jnp.stack([blocks[i].astype(bf16) for i in sent]), bit)
            for at, i in enumerate(sent):
                blocks[i ^ bit] = blocks[i ^ bit].astype(f32) + got[at].astype(f32)
                del blocks[i]
        return blocks[0]

    prompt_keys = jnp.concatenate(exchange(key_rows[:prompt_rows], slab_bits), axis=0)
    prompt_values = jnp.concatenate(exchange(value_rows[:prompt_rows], slab_bits[::-1]), axis=0)
    key_own, value_own = key_rows[prompt_rows:], value_rows[prompt_rows:]
    def experts_of_sets(x, axes):
        count, width_x = lax.axis_size(axes), x.shape[3]
        x = x.reshape(sets_local, shard_count, -1, width_x).transpose(1, 0, 2, 3)
        x = x.reshape(shard_count, count, -1, width_x)
        got = []
        for s in range(shard_count):
            at = ((shard_index - s) % shard_count, lax.axis_index(axes), 0, 0)
            block = lax.dynamic_slice(x, at, (1, 1) + x.shape[2:])[0, 0]
            got.append(from_shard(block, s) if s else block)
        return jnp.stack(got)

    def gather_adapters(x, axes):
        whole = lax.all_gather(x, axes, axis=1, tiled=True)
        return whole.reshape(SETS, -1, x.shape[2])

    def sets_of_experts(x, axes):
        width_x = x.shape[2]
        x = x.astype(bf16).reshape(shard_count, -1, width_x)
        mine = lax.psum_scatter(x, axes, scatter_dimension=1, tiled=True)
        got = [to_shard(mine[s], s) if s else mine[s] for s in range(shard_count)]
        whole = lax.all_gather(by_shard(got, shard_index - shard_at), axes, axis=1, tiled=True)
        return whole.reshape(shard_count, sets_local, locals_n, -1, width_x).transpose(1, 0, 2, 3, 4)

    wide = jnp.concatenate(
        [gu_a.transpose(0, 1, 3, 4, 2).reshape(sets_local, EXPERTS, -1, full_width), down_b], axis=2
    )
    slim = jnp.concatenate(
        [
            gu_b.transpose(0, 1, 3, 2, 4).reshape(sets_local, EXPERTS, -1, ff_local),
            down_a.transpose(0, 1, 3, 2),
        ],
        axis=2,
    )
    wide = experts_of_sets(wide, ("ctx", "tp"))
    slim = experts_of_sets(slim, ("ctx",))
    cot_got = [from_shard(cot_mine, s) for s in range(1, shard_count)]
    query_rows, wide, slim = lax.optimization_barrier((query_rows, wide, slim))
    wide = gather_adapters(wide, ("ctx", "tp"))
    slim = gather_adapters(slim, ("ctx",))
    attention_rows, log_total = attention_forward(
        slab, query_rows, prompt_keys, prompt_values, key_own, value_own, prompt_rows
    )
    attention_rows, cot_got = lax.optimization_barrier((attention_rows, cot_got))
    whole_out = lax.all_gather(my_slab(w_out, 1), ("fsdp", "ctx"), axis=1, tiled=True)
    mid_out = (
        ADAPTER_SCALE
        * jnp.einsum("tnd,trd->tnr", tile_rows(attention_rows), t_out_a, preferred_element_type=f32)
    ).astype(bf16)
    branch = sum_parts(
        jnp.dot(attention_rows, whole_out, preferred_element_type=f32)
        + jnp.einsum("tnr,trd->tnd", mid_out, t_out_b, preferred_element_type=f32).reshape(
            row_count, full_width
        )
    )
    x_mid = token_vals + branch
    mid_scale = lax.rsqrt(jnp.mean(x_mid * x_mid, axis=1, keepdims=True) + epsilon)
    h_second = (x_mid * mid_scale * gain_mid).astype(bf16)
    h_tiles = tile_rows(h_second)
    mid_router = (
        ADAPTER_SCALE
        * jnp.einsum("tnd,trd->tnr", h_tiles, t_router_a, preferred_element_type=f32)
    ).astype(bf16)
    router_logits = jnp.dot(h_second, w_router, preferred_element_type=f32) + jnp.einsum(
        "tnr,tre->tne", mid_router, t_router_b, preferred_element_type=f32
    ).reshape(row_count, EXPERTS)
    expert_probs = jax.nn.softmax(router_logits, axis=1)
    chosen = jnp.any(
        routes[:, :, None] == jnp.arange(EXPERTS, dtype=jnp.int32)[None, None, :], axis=1
    )
    gates = jnp.where(chosen, expert_probs, 0.0)

    gu_rank = 2 * RANK
    adapters = (wide, slim)
    sums = tuple(jnp.zeros(a.shape, f32) for a in adapters)
    w_gu = w_gate_up.transpose(0, 2, 1, 3)
    part = part_index.reshape(1).astype(jnp.int32)
    h_mine = my_part(h_second)
    cot_steps = [cotangent] + [(x, swap(x)) for x in cot_got]
    gates_t = gates.T
    gate_steps = []
    for s in range(shard_count):
        block = lax.dynamic_slice_in_dim(
            gates_t, ((shard_index - s) % shard_count) * locals_n, locals_n, axis=0
        )
        gate_steps.append((from_shard(block, s) if s else block).T)
    y_steps, dh_steps, d_gate_steps = [], [], []
    h_step = h_second
    h_next = from_shard(h_mine, 1)
    for s in range(shard_count):
        y_keep, y_send, dh_keep, dh_send, d_gate, *sums = expert_pass(
            step_order[s], step_order_sets[s], part, h_step, cot_steps[s], gate_steps[s], w_gu,
            w_down, adapters, tuple(sums),
        )
        dh = dh_keep.astype(f32) + swap(dh_send).astype(f32)
        if s:
            dh = dh.astype(bf16)
        if s + 1 < shard_count:
            h_step = (h_next, swap(h_next))
            sums, h_step, h_mine, dh, dh_steps = lax.optimization_barrier(
                (sums, h_step, h_mine, dh, dh_steps)
            )
            if s + 2 < shard_count:
                h_next = from_shard(h_mine, s + 2)
        dh_steps.append(to_shard(dh, s) if s else dh)
        d_gate = d_gate.T
        d_gate_steps.append(to_shard(d_gate, s) if s else d_gate)
        y_steps.append((y_keep, y_send))
    d_gates = sum_parts(
        by_shard(d_gate_steps, shard_index - shard_at).reshape(EXPERTS, row_count)
    ).T
    d_second_mine = sum(dh.astype(f32) for dh in dh_steps).astype(bf16)
    y_steps = [keep.astype(f32) + swap(send).astype(f32) for keep, send in y_steps]
    y_steps = [y.astype(bf16) if s else y for s, y in enumerate(y_steps)]
    d_second_mine, y_steps = lax.optimization_barrier((d_second_mine, y_steps))
    d_second_routed = join_parts(d_second_mine, swap(d_second_mine)).astype(f32)
    y_odd = [to_shard(y_steps[s], s) for s in range(1, shard_count, 2)]

    d_probs = jnp.where(chosen, d_gates, 0.0)
    d_logits = (
        expert_probs * (d_probs - jnp.sum(expert_probs * d_probs, axis=1, keepdims=True))
    ).astype(bf16)
    dl_tiles = tile_rows(d_logits)
    d_mid_router = (
        ADAPTER_SCALE
        * jnp.einsum("tne,tre->tnr", dl_tiles, t_router_b, preferred_element_type=f32)
    ).astype(bf16)
    g_router_b = jnp.einsum("tnr,tne->tre", mid_router, dl_tiles, preferred_element_type=f32)
    g_router_a = jnp.einsum("tnr,tnd->trd", d_mid_router, h_tiles, preferred_element_type=f32)
    d_second = (
        d_second_routed
        + jnp.einsum("ne,de->nd", d_logits, w_router, preferred_element_type=f32)
        + jnp.einsum("tnr,trd->tnd", d_mid_router, t_router_a, preferred_element_type=f32).reshape(
            row_count, full_width
        )
    )
    d_x_mid = cot_vals + rms_back(x_mid, gain_mid, d_second, mid_scale, full_width)
    d_branch = d_x_mid.astype(bf16)
    db_tiles = tile_rows(d_branch)
    d_mid_out = (
        ADAPTER_SCALE
        * jnp.einsum("tnd,trd->tnr", db_tiles, t_out_b, preferred_element_type=f32)
    ).astype(bf16)
    d_att = jnp.einsum("nc,oc->no", d_branch, whole_out, preferred_element_type=f32) + jnp.einsum(
        "tnr,tro->tno", d_mid_out, t_out_a, preferred_element_type=f32
    ).reshape(row_count, local_width)
    g_out_b = jnp.einsum("tnr,tnd->trd", mid_out, db_tiles, preferred_element_type=f32)
    g_out_a = jnp.einsum(
        "tnr,tno->tro", d_mid_out, tile_rows(attention_rows), preferred_element_type=f32
    )
    d_att_rows = d_att.astype(bf16)
    d_query, d_key_all, d_value_all, d_key_own, d_value_own = attention_backward(
        slab, query_rows, prompt_keys, prompt_values, key_own, value_own, attention_rows,
        d_att_rows, log_total, prompt_rows,
    )
    d_query, y_odd, y_steps = lax.optimization_barrier((d_query, y_odd, y_steps))
    y_even = [to_shard(y_steps[s], s) for s in range(2, shard_count, 2)]
    d_key_prompt = exchange_back(d_key_all, slab_bits)
    d_value_prompt = exchange_back(d_value_all, slab_bits[::-1])
    d_key = jnp.concatenate([d_key_prompt, d_key_own], axis=0)
    d_value = jnp.concatenate([d_value_prompt, d_value_own], axis=0)
    d_q_norm = rotate(heads_of(d_query), cosine, -sine_part).reshape(row_count, local_width)
    d_k_norm = rotate(heads_of(d_key), cosine, -sine_part).reshape(row_count, local_width)
    dots = sum_parts(
        jnp.stack(
            [jnp.sum(gain_q * q_raw * d_q_norm, axis=1), jnp.sum(gain_k * k_raw * d_k_norm, axis=1)]
        )
    )
    d_q_raw = (
        q_scale * gain_q * d_q_norm
        - q_raw * (q_scale * q_scale * q_scale) * dots[0][:, None] / full_width
    )
    d_k_raw = (
        k_scale * gain_k * d_k_norm
        - k_raw * (k_scale * k_scale * k_scale) * dots[1][:, None] / full_width
    )
    d_proj = jnp.stack([d_q_raw, d_k_raw, d_value], axis=0).astype(bf16)
    d_proj, y_even = lax.optimization_barrier((d_proj, y_even))
    mixed_mine = sum(
        [y.astype(f32) for y in y_steps[:1] + y_odd + y_even], my_part(x_mid)
    ).astype(bf16)
    mixed = join_parts(mixed_mine, swap(mixed_mine))
    dp_tiles = d_proj.reshape(3, tiles, TILE, local_width)
    d_mid_qkv = (
        ADAPTER_SCALE
        * jnp.einsum("jtno,tjro->tnjr", dp_tiles, t_qkv_b, preferred_element_type=f32)
    ).astype(bf16)
    d_first = sum_parts(
        sum(dot_nt(d_proj[j], weights[j]) for j in range(3))
        + jnp.einsum("tnjr,tjrd->tnd", d_mid_qkv, t_qkv_a, preferred_element_type=f32).reshape(
            row_count, full_width
        )
    )
    grad_input = d_x_mid + rms_back(token_vals, gain_in, d_first, first_scale, full_width)
    g_qkv_b = jnp.einsum("tnjr,jtno->tjro", mid_qkv, dp_tiles, preferred_element_type=f32)
    g_qkv_a = jnp.einsum(
        "tnjr,tnd->tjrd", d_mid_qkv, tile_rows(h_first), preferred_element_type=f32
    )

    def to_sets(pieces_):
        rows_ = jnp.concatenate(pieces_, axis=1)
        return jnp.sum(tile_hot[:, :, None, None] * rows_[None], axis=1)

    def reduced(x):
        n_rows = x.shape[1]
        pad = -n_rows % (16 * slab_count)
        x = jnp.pad(x.astype(bf16), ((0, 0), (0, pad), (0, 0)))
        x = x.reshape(shard_count, sets_local, slab_count, -1, local_width)
        x = x.transpose(0, 2, 1, 3, 4).reshape((shard_count * slab_count, sets_local, -1, local_width))
        mine = lax.psum_scatter(x, ("fsdp", "ctx"), scatter_dimension=0, tiled=False)
        return lax.all_gather(mine, "ctx", axis=1, tiled=True)[:, :n_rows].astype(f32)

    early_both = sum_parts(to_sets([as_rows(g_out_b)]))
    early_one = to_sets([as_rows(g_out_a), as_rows(g_router_a), router_rows(g_router_b)])
    early = reduced(jnp.concatenate([early_both, early_one], axis=1))
    late_both = sum_parts(to_sets([as_rows(g_qkv_a)]))
    late = reduced(jnp.concatenate([late_both, to_sets([as_rows(g_qkv_b)])], axis=1))
    n0, n2, n3, n4 = sizes[0], sizes[2], sizes[3], sizes[4]
    grad_qkv_a = late[:, :n0].reshape(sets_local, 3, RANK, full_width).transpose(0, 3, 1, 2)
    grad_qkv_b = late[:, n0:].reshape(sets_local, 3, RANK, local_width).transpose(0, 2, 1, 3)
    grad_out_b = early[:, :n3].reshape(out_b.shape)
    grad_out_a = early[:, n3 : n3 + n2].reshape(sets_local, RANK, local_width).transpose(0, 2, 1)
    grad_router_a = (
        early[:, n3 + n2 : n3 + n2 + n4].reshape(sets_local, RANK, full_width).transpose(0, 2, 1)
    )
    grad_router_b = early[:, n3 + n2 + n4, : RANK * EXPERTS].reshape(router_b.shape)

    g_wide = sets_of_experts(sums[0], ("ctx", "tp"))
    g_slim = sets_of_experts(sums[1], ("ctx",))

    def of_experts(g):
        return g.reshape((sets_local, EXPERTS) + g.shape[3:]).astype(f32)

    grad_gu_a = (
        of_experts(g_wide[:, :, :, :gu_rank])
        .reshape(sets_local, EXPERTS, 2, RANK, full_width)
        .transpose(0, 1, 4, 2, 3)
    )
    grad_gu_b = (
        of_experts(g_slim[:, :, :, :gu_rank])
        .reshape(sets_local, EXPERTS, 2, RANK, ff_local)
        .transpose(0, 1, 3, 2, 4)
    )
    grad_down_a = of_experts(g_slim[:, :, :, gu_rank:]).transpose(0, 1, 3, 2)
    grad_down_b = of_experts(g_wide[:, :, :, gu_rank:])
    return (
        mixed, grad_input, grad_qkv_a, grad_qkv_b, grad_out_a, grad_out_b, grad_router_a,
        grad_router_b, grad_gu_a, grad_gu_b, grad_down_a, grad_down_b,
    )


def solution(mesh):
    return jax.shard_map(
        per_device,
        mesh=mesh,
        in_specs=(
            P(("fsdp", "ctx"), None),
            P(("fsdp", "ctx"), None),
            P(("fsdp", "ctx"), None),
            P("fsdp", None),
            P(),
            P(),
            P("tp"),
            P("tp"),
            P("fsdp", None, "tp"),
            P("tp", "fsdp"),
            P(),
            P("fsdp", None, None, "tp"),
            P("fsdp", "tp", None),
            P("fsdp", None, None, None),
            P("fsdp", None, None, "tp"),
            P("fsdp", "tp", None),
            P("fsdp", None, None),
            P("fsdp", None, None),
            P("fsdp", None, None),
            P("fsdp", None, None, None, None),
            P("fsdp", None, None, None, "tp"),
            P("fsdp", None, "tp", None),
            P("fsdp", None, None, None),
        ),
        out_specs=(
            P(("fsdp", "ctx"), None),
            P(("fsdp", "ctx"), None),
            P("fsdp", None, None, None),
            P("fsdp", None, None, "tp"),
            P("fsdp", "tp", None),
            P("fsdp", None, None),
            P("fsdp", None, None),
            P("fsdp", None, None),
            P("fsdp", None, None, None, None),
            P("fsdp", None, None, None, "tp"),
            P("fsdp", None, "tp", None),
            P("fsdp", None, None, None),
        ),
        check_vma=False,
    )
```

```python
import jax
import jax.numpy as jnp
from jax import lax
from jax.experimental import pallas as pl
from jax.experimental.pallas import tpu as pltpu
from jax.sharding import PartitionSpec as P

HEAD_DIM = 128
TOPK = 8
EXPERTS = 16
RANK = 16
PROMPT = 2048
CONT_LEN = 256
CONTS = 8
SETS = 8

epsilon = 1e-05
ADAPTER_SCALE = 0.5
ROPE_BASE = 10000.0
masked_score = -1e30
TILE = CONT_LEN
SCORE_SCALE = HEAD_DIM ** (-0.5)
f32 = jnp.float32
bf16 = jnp.bfloat16


def dot_nn(a, b):
    return lax.dot_general(a, b, (((1,), (0,)), ((), ())), preferred_element_type=f32)


def dot_nt(a, b):
    return lax.dot_general(a, b, (((1,), (1,)), ((), ())), preferred_element_type=f32)


def dot_tn(a, b):
    return lax.dot_general(a, b, (((0,), (0,)), ((), ())), preferred_element_type=f32)


def rms_back(value, gain, grad, scale_col, full_width):
    inner = jnp.sum(gain * value * grad, axis=-1, keepdims=True)
    return (
        scale_col * gain * grad - value * (scale_col * scale_col * scale_col) * inner / full_width
    )


def angles(positions):
    freqs = ROPE_BASE ** (-(2.0 * jnp.arange(HEAD_DIM // 2, dtype=f32)) / HEAD_DIM)
    turned = positions.astype(f32)[:, None] * freqs[None, :]
    return (jnp.cos(turned)[:, None, :], jnp.sin(turned)[:, None, :])


def rotate(value, cosine, sine_part):
    half_dim = value.shape[-1] // 2
    first_half = value[..., :half_dim]
    second_half = value[..., half_dim:]
    return jnp.concatenate(
        [
            first_half * cosine - second_half * sine_part,
            second_half * cosine + first_half * sine_part,
        ],
        axis=-1,
    )


def attention_scores(k_ref, q, slab_ref, tile, prompt_rows, is_prompt):
    scores = dot_nt(k_ref[...], q) * SCORE_SCALE
    if not is_prompt:
        return scores
    block_at = lax.broadcasted_iota(jnp.int32, (prompt_rows, scores.shape[1]), 0)
    key_at = jnp.concatenate(
        [
            block_at + jnp.bitwise_xor(slab_ref[0], b) * prompt_rows
            for b in range(scores.shape[0] // prompt_rows)
        ],
        axis=0,
    )
    query_at = (
        slab_ref[0] * prompt_rows + tile * TILE + lax.broadcasted_iota(jnp.int32, scores.shape, 1)
    )
    return jnp.where(key_at <= query_at, scores, masked_score)


def own_scores(ko_ref, q):
    scores = dot_nt(ko_ref[...], q) * SCORE_SCALE
    key_at = lax.broadcasted_iota(jnp.int32, scores.shape, 0)
    query_at = lax.broadcasted_iota(jnp.int32, scores.shape, 1)
    return jnp.where(key_at <= query_at, scores, masked_score)


def attention_forward(slab, q, k, v, ko, vo, prompt_rows):
    rows, width = q.shape
    heads, tiles, prompt_tiles = width // HEAD_DIM, rows // TILE, prompt_rows // TILE
    keys = k.shape[0]

    def body(slab_ref, q_ref, k_ref, v_ref, ko_ref, vo_ref, att_ref, lse_ref, vt_ref):
        tile = pl.program_id(1)

        @pl.when(tile == 0)
        def _():
            vt_ref[...] = v_ref[...].T

        query = q_ref[...]

        def finish(total, peak, out_t):
            att_ref[...] = (out_t / total).T.astype(bf16)
            lse_ref[0] = peak + jnp.log(total)

        @pl.when(tile < prompt_tiles)
        def _():
            scores = attention_scores(k_ref, query, slab_ref, tile, prompt_rows, True)
            peak = jnp.max(scores, axis=0, keepdims=True)
            probs = jnp.exp(scores - peak)
            total = jnp.sum(probs, axis=0, keepdims=True)
            finish(total, peak, dot_nn(vt_ref[...], probs.astype(bf16)))

        @pl.when(tile >= prompt_tiles)
        def _():
            scores = attention_scores(k_ref, query, slab_ref, tile, prompt_rows, False)
            own = own_scores(ko_ref, query)
            peak = jnp.maximum(
                jnp.max(scores, axis=0, keepdims=True), jnp.max(own, axis=0, keepdims=True)
            )
            probs = jnp.exp(scores - peak)
            own_probs = jnp.exp(own - peak)
            total = jnp.sum(probs, axis=0, keepdims=True) + jnp.sum(
                own_probs, axis=0, keepdims=True
            )
            out_t = dot_nn(vt_ref[...], probs.astype(bf16)) + dot_nn(
                vo_ref[...].T, own_probs.astype(bf16)
            )
            finish(total, peak, out_t)

    tile_spec = pl.BlockSpec((TILE, HEAD_DIM), lambda h, t, s: (t, h))
    key_spec = pl.BlockSpec((keys, HEAD_DIM), lambda h, t, s: (0, h))
    own_spec = pl.BlockSpec(
        (TILE, HEAD_DIM), lambda h, t, s: (jnp.maximum(t - prompt_tiles, 0), h)
    )
    return pl.pallas_call(
        body,
        grid_spec=pltpu.PrefetchScalarGridSpec(
            num_scalar_prefetch=1,
            grid=(heads, tiles),
            in_specs=[tile_spec, key_spec, key_spec, own_spec, own_spec],
            out_specs=[tile_spec, pl.BlockSpec((1, 1, TILE), lambda h, t, s: (h, 0, t))],
            scratch_shapes=[pltpu.VMEM((HEAD_DIM, keys), bf16)],
        ),
        out_shape=[
            jax.ShapeDtypeStruct((rows, width), bf16),
            jax.ShapeDtypeStruct((heads, 1, rows), f32),
        ],
        compiler_params=pltpu.CompilerParams(
            dimension_semantics=("arbitrary", "arbitrary"), vmem_limit_bytes=56 << 20
        ),
        name="attention_forward",
    )(slab, q, k, v, ko, vo)


def attention_backward(slab, q, k, v, ko, vo, att, d_att, lse, prompt_rows):
    rows, width = q.shape
    heads, tiles, prompt_tiles = width // HEAD_DIM, rows // TILE, prompt_rows // TILE
    keys = k.shape[0]

    def body(
        slab_ref, q_ref, k_ref, v_ref, ko_ref, vo_ref, att_ref, da_ref, lse_ref,
        dq_ref, dk_ref, dv_ref, dko_ref, dvo_ref, kt_ref, dka_ref, dva_ref,
    ):
        tile = pl.program_id(1)

        @pl.when(tile == 0)
        def _():
            kt_ref[...] = k_ref[...].T
            dka_ref[...] = jnp.zeros_like(dka_ref)
            dva_ref[...] = jnp.zeros_like(dva_ref)

        query = q_ref[...]
        d_out = da_ref[...]
        delta = jnp.sum(
            (d_out.astype(f32) * att_ref[...].astype(f32)).T, axis=0, keepdims=True
        )
        log_total = lse_ref[0]

        def prompt_keys(is_prompt):
            scores = attention_scores(k_ref, query, slab_ref, tile, prompt_rows, is_prompt)
            probs = jnp.exp(scores - log_total)
            d_probs = dot_nt(v_ref[...], d_out)
            d_scores = (probs * (d_probs - delta)).astype(bf16)
            dka_ref[...] += dot_nn(d_scores, query)
            dva_ref[...] += dot_nn(probs.astype(bf16), d_out)
            return dot_nn(kt_ref[...], d_scores)

        @pl.when(tile < prompt_tiles)
        def _():
            dq_ref[...] = prompt_keys(True).T * SCORE_SCALE

        @pl.when(tile >= prompt_tiles)
        def _():
            dq_t = prompt_keys(False)
            probs = jnp.exp(own_scores(ko_ref, query) - log_total)
            d_probs = dot_nt(vo_ref[...], d_out)
            d_scores = (probs * (d_probs - delta)).astype(bf16)
            dko_ref[...] = dot_nn(d_scores, query) * SCORE_SCALE
            dvo_ref[...] = dot_nn(probs.astype(bf16), d_out)
            dq_ref[...] = (dq_t + dot_nn(ko_ref[...].T, d_scores)).T * SCORE_SCALE

        @pl.when(tile == tiles - 1)
        def _():
            dk_ref[...] = (dka_ref[...] * SCORE_SCALE).astype(bf16)
            dv_ref[...] = dva_ref[...].astype(bf16)

    tile_spec = pl.BlockSpec((TILE, HEAD_DIM), lambda h, t, s: (t, h))
    key_spec = pl.BlockSpec((keys, HEAD_DIM), lambda h, t, s: (0, h))
    own_spec = pl.BlockSpec(
        (TILE, HEAD_DIM), lambda h, t, s: (jnp.maximum(t - prompt_tiles, 0), h)
    )
    return pl.pallas_call(
        body,
        grid_spec=pltpu.PrefetchScalarGridSpec(
            num_scalar_prefetch=1,
            grid=(heads, tiles),
            in_specs=[
                tile_spec, key_spec, key_spec, own_spec, own_spec, tile_spec, tile_spec,
                pl.BlockSpec((1, 1, TILE), lambda h, t, s: (h, 0, t)),
            ],
            out_specs=[tile_spec, key_spec, key_spec, own_spec, own_spec],
            scratch_shapes=[
                pltpu.VMEM((HEAD_DIM, keys), bf16),
                pltpu.VMEM((keys, HEAD_DIM), f32),
                pltpu.VMEM((keys, HEAD_DIM), f32),
            ],
        ),
        out_shape=[
            jax.ShapeDtypeStruct((rows, width), f32),
            jax.ShapeDtypeStruct((keys, width), bf16),
            jax.ShapeDtypeStruct((keys, width), bf16),
            jax.ShapeDtypeStruct((rows - prompt_rows, width), f32),
            jax.ShapeDtypeStruct((rows - prompt_rows, width), f32),
        ],
        compiler_params=pltpu.CompilerParams(
            dimension_semantics=("arbitrary", "arbitrary"), vmem_limit_bytes=56 << 20
        ),
        name="attention_backward",
    )(slab, q, k, v, ko, vo, att, d_att, lse)


def expert_pass(order, order_sets, part, h, cot, gates, w_gu, w_dn, adapters, sums):
    halved = isinstance(h, tuple)
    rows = h[0].shape[0] if halved else h.shape[0]
    width = w_gu.shape[2]
    part_width = width // 2
    locals_n = gates.shape[1]
    tiles = rows // TILE

    def body(
        order_ref, set_ref, part_ref, h0_ref, h1_ref, cot0_ref, cot1_ref, gate_ref, wgu_ref,
        wdn_ref, wide_ref, slim_ref, swide_ref, sslim_ref,
        yk_ref, ys_ref, dhk_ref, dhs_ref, dgate_ref, gwide_ref, gslim_ref,
        y_acc, dh_acc, x_ref, ct_ref, n_ref, mid_ref,
    ):
        step = pl.program_id(0)
        fresh = jnp.logical_or(
            step == 0, set_ref[step] != set_ref[jnp.maximum(step - 1, 0)]
        )

        @pl.when(fresh)
        def _():
            gwide_ref[...] = swide_ref[...]
            gslim_ref[...] = sslim_ref[...]

        low_first = part_ref[0] == 0

        def join(first, second):
            x_ref[:, :part_width] = h0_ref[...] if first else h1_ref[...]
            x_ref[:, part_width:] = h1_ref[...] if first else h0_ref[...]
            ct_ref[:, :part_width] = cot0_ref[...] if first else cot1_ref[...]
            ct_ref[:, part_width:] = cot1_ref[...] if first else cot0_ref[...]

        if halved:
            pl.when(low_first)(lambda: join(True, False))
            pl.when(jnp.logical_not(low_first))(lambda: join(False, True))
        else:
            join(True, False)
        x = x_ref[...]
        ct = ct_ref[...]
        wide = wide_ref[0]
        slim = slim_ref[0]
        lane = lax.broadcasted_iota(jnp.int32, (TILE, wide.shape[0]), 1)
        mid_gu = (ADAPTER_SCALE * dot_nt(x, wide)).astype(bf16)
        d_mid_dn = (ADAPTER_SCALE * dot_nt(ct, wide)).astype(bf16)
        zero_mid = jnp.zeros_like(mid_gu)
        n_ref[...] = jnp.zeros_like(n_ref)
        mid_ref[...] = jnp.zeros_like(mid_ref)
        y_acc[...] = jnp.zeros_like(y_acc)
        dh_acc[...] = jnp.zeros_like(dh_acc)
        gate_block = gate_ref[...]
        gate_lane = lax.broadcasted_iota(jnp.int32, gate_block.shape, 1)

        def expert(e, d_gates):
            gate_lanes = (lane // RANK) == 3 * e
            up_lanes = (lane // RANK) == 3 * e + 1
            dn_lanes = (lane // RANK) == 3 * e + 2
            mid_gate = jnp.where(gate_lanes, mid_gu, zero_mid)
            mid_up = jnp.where(up_lanes, mid_gu, zero_mid)
            d_mid_e = jnp.where(dn_lanes, d_mid_dn, zero_mid)
            g = dot_nn(x_ref[...], wgu_ref[e, 0]) + dot_nn(mid_gate, slim)
            u = dot_nn(x_ref[...], wgu_ref[e, 1]) + dot_nn(mid_up, slim)
            c = dot_nt(ct_ref[...], wdn_ref[e]) + dot_nn(d_mid_e, slim)
            gate = jnp.sum(jnp.where(gate_lane == e, gate_block, 0.0), axis=1, keepdims=True)
            sig = jax.nn.sigmoid(g)
            silu = g * sig
            hidden = silu * u
            hidden_b = hidden.astype(bf16)
            d_gate = jnp.sum(hidden_b.astype(f32) * c, axis=1, keepdims=True)
            d_hidden = gate * c
            d_g = (d_hidden * u * sig * (1.0 + g * (1.0 - sig))).astype(bf16)
            d_u = (d_hidden * silu).astype(bf16)
            gated = (gate * hidden).astype(bf16)
            y_acc[...] += dot_nn(gated, wdn_ref[e])
            dh_acc[...] += dot_nt(d_g, wgu_ref[e, 0]) + dot_nt(d_u, wgu_ref[e, 1])
            mid_ref[...] = jnp.where(dn_lanes, dot_nt(gated, slim), mid_ref[...])
            n_e = jnp.where(gate_lanes, dot_nt(d_g, slim), n_ref[...])
            n_ref[...] = jnp.where(up_lanes, dot_nt(d_u, slim), n_e)
            gslim_ref[0] += (
                dot_tn(mid_gate, d_g)
                + dot_tn(mid_up, d_u)
                + dot_tn((gate * d_mid_e.astype(f32)).astype(bf16), hidden_b)
            )
            return jnp.where(gate_lane == e, d_gate, d_gates)

        dgate_ref[...] = lax.fori_loop(0, locals_n, expert, jnp.zeros(gate_block.shape, f32))
        n_b = (ADAPTER_SCALE * n_ref[...]).astype(bf16)
        mid_dn_b = (ADAPTER_SCALE * mid_ref[...]).astype(bf16)
        y = (y_acc[...] + dot_nn(mid_dn_b, wide)).astype(bf16)
        dh = (dh_acc[...] + dot_nn(n_b, wide)).astype(bf16)

        def part_out(keep_low):
            low, high = slice(0, part_width), slice(part_width, width)
            keep, send = (low, high) if keep_low else (high, low)
            yk_ref[...] = y[:, keep]
            ys_ref[...] = y[:, send]
            dhk_ref[...] = dh[:, keep]
            dhs_ref[...] = dh[:, send]

        pl.when(low_first)(lambda: part_out(True))
        pl.when(jnp.logical_not(low_first))(lambda: part_out(False))
        gwide_ref[0] += dot_tn(n_b, x) + dot_tn(mid_dn_b, ct)

    def row_spec(column):
        return pl.BlockSpec((TILE, part_width), lambda i, o, s, p: (o[i], column))

    gate_spec = pl.BlockSpec((TILE, locals_n), lambda i, o, s, p: (o[i], 0))

    def whole(a):
        zeros = (0,) * a.ndim
        return pl.BlockSpec(a.shape, lambda i, o, s, p: zeros, pipeline_mode=pl.Buffered(1))

    def of_set(a):
        return pl.BlockSpec((1,) + a.shape[1:], lambda i, o, s, p: (s[i], 0, 0))

    if halved:
        row_args = h + cot
        row_specs = [row_spec(0)] * 4
    else:
        row_args = (h, h, cot, cot)
        row_specs = [row_spec(0), row_spec(1)] * 2
    half = jax.ShapeDtypeStruct((rows, part_width), bf16)
    return pl.pallas_call(
        body,
        grid_spec=pltpu.PrefetchScalarGridSpec(
            num_scalar_prefetch=3,
            grid=(tiles,),
            in_specs=row_specs + [gate_spec, whole(w_gu), whole(w_dn)]
            + [of_set(a) for a in adapters] + [of_set(a) for a in sums],
            out_specs=[row_spec(0)] * 4 + [gate_spec] + [of_set(a) for a in sums],
            scratch_shapes=[
                pltpu.VMEM((TILE, width), f32), pltpu.VMEM((TILE, width), f32),
                pltpu.VMEM((TILE, width), bf16), pltpu.VMEM((TILE, width), bf16),
                pltpu.VMEM((TILE, adapters[0].shape[1]), f32),
                pltpu.VMEM((TILE, adapters[0].shape[1]), f32),
            ],
        ),
        out_shape=[half] * 4 + [jax.ShapeDtypeStruct(gates.shape, f32)]
        + [jax.ShapeDtypeStruct(a.shape, f32) for a in sums],
        input_output_aliases={12 + i: 5 + i for i in range(2)},
        compiler_params=pltpu.CompilerParams(
            dimension_semantics=("arbitrary",), vmem_limit_bytes=60 << 20
        ),
        name="expert_pass",
    )(order, order_sets, part, *row_args, gates, w_gu, w_dn, *adapters, *sums)


def per_device(
    tokens, cotangent, routes, adapter_ids, norm_in, norm_mid, q_gain, k_gain, w_qkv, w_out,
    w_router, w_gate_up, w_down, qkv_a, qkv_b, out_a, out_b, router_a, router_b, gu_a, gu_b,
    down_a, down_b,
):
    row_count, full_width = tokens.shape
    local_width = q_gain.shape[0]
    local_heads = local_width // HEAD_DIM
    locals_n, ff_local = w_gate_up.shape[0], w_gate_up.shape[3]
    shard_count, slab_count, part_count = (
        lax.axis_size("fsdp"), lax.axis_size("ctx"), lax.axis_size("tp"),
    )
    shard_index, slab_index, part_index = (
        lax.axis_index("fsdp"), lax.axis_index("ctx"), lax.axis_index("tp"),
    )
    part_width = full_width // part_count
    prompt_rows = PROMPT // slab_count
    cont_count = CONTS // slab_count
    tiles, prompt_tiles = row_count // TILE, prompt_rows // TILE
    row_index = jnp.arange(row_count, dtype=jnp.int32)
    tail_offset = jnp.maximum(row_index - prompt_rows, 0)
    leading = row_index < prompt_rows
    positions = jnp.where(
        leading, slab_index * prompt_rows + row_index, PROMPT + tail_offset % CONT_LEN
    )
    cosine, sine_part = angles(positions)
    slab = slab_index.reshape(1).astype(jnp.int32)

    def my_part(x):
        return lax.dynamic_slice_in_dim(x, part_index * part_width, part_width, axis=1)

    def tile_rows(x):
        return x.reshape(tiles, TILE, x.shape[1])

    def from_shard(x, s):
        return lax.ppermute(
            x, "fsdp", [(i, (i - s) % shard_count) for i in range(shard_count)]
        )

    def to_shard(x, s):
        return lax.ppermute(
            x, "fsdp", [(i, (i + s) % shard_count) for i in range(shard_count)]
        )

    def swap(x):
        return lax.ppermute(x, "tp", [(0, 1), (1, 0)])

    def across(x, bit):
        return lax.ppermute(x, "ctx", [(i, i ^ bit) for i in range(slab_count)])

    def sum_parts(x):
        return x + swap(x)

    def join_parts(mine, other):
        low_first = part_index == 0
        return jnp.concatenate(
            [jnp.where(low_first, mine, other), jnp.where(low_first, other, mine)], axis=1
        )

    def my_slab(x, axis):
        size = x.shape[axis] // slab_count
        return lax.dynamic_slice_in_dim(x, slab_index * size, size, axis=axis)

    def by_shard(pieces_, index):
        return jnp.take(jnp.stack(pieces_), index % shard_count, axis=0)

    shard_at = jnp.arange(shard_count, dtype=jnp.int32)
    slab_bits = [1 << i for i in range(slab_count.bit_length() - 1)]

    cont_sets = lax.dynamic_slice_in_dim(adapter_ids[0], 1 + slab_index * cont_count, cont_count)
    tile_sets = jnp.concatenate([jnp.broadcast_to(adapter_ids[0, :1], (prompt_tiles,)), cont_sets])
    step_sets = jnp.stack([tile_sets] + [from_shard(tile_sets, s) for s in range(1, shard_count)])
    sets_local = qkv_a.shape[0]
    step_sets = (
        (step_sets // sets_local - shard_index) % shard_count * sets_local + step_sets % sets_local
    )
    tile_at = jnp.arange(tiles, dtype=jnp.int32)
    left, right = step_sets[:, None, :], step_sets[:, :, None]
    ahead = (left < right) | ((left == right) & (tile_at[None, None, :] < tile_at[None, :, None]))
    rank_of = jnp.sum(ahead.astype(jnp.int32), axis=2)
    at_rank = (rank_of[:, None, :] == tile_at[None, :, None]).astype(jnp.int32)
    step_order = jnp.sum(at_rank * tile_at[None, None, :], axis=2)
    step_order_sets = jnp.sum(at_rank * left, axis=2)
    set_at = jnp.arange(SETS, dtype=jnp.int32)
    tile_hot = (set_at[:, None] == tile_sets[None, :]).astype(f32)


    def as_rows(x):
        return x.reshape(x.shape[0], -1, local_width)

    def router_rows(x):
        flat = x.reshape(x.shape[0], 1, -1)
        return jnp.pad(flat, ((0, 0), (0, 0), (0, local_width - flat.shape[2])))

    pieces = [
        as_rows(qkv_a.transpose(0, 2, 3, 1)),
        as_rows(qkv_b.transpose(0, 2, 1, 3)),
        as_rows(out_a.transpose(0, 2, 1)),
        as_rows(out_b),
        as_rows(router_a.transpose(0, 2, 1)),
        router_rows(router_b),
    ]
    sizes = [p.shape[1] for p in pieces]
    rows_n = sum(sizes)
    rows_pad = -rows_n % (16 * slab_count)
    packed = my_slab(
        jnp.pad(jnp.concatenate(pieces, axis=1), ((0, 0), (0, rows_pad), (0, 0))), 1
    )
    packed = lax.all_gather(packed, ("fsdp", "ctx"), axis=0, tiled=False)
    packed = packed.reshape((shard_count, slab_count) + packed.shape[1:]).transpose(0, 2, 1, 3, 4)
    packed = packed.reshape(SETS, rows_n + rows_pad, local_width)
    picked = jnp.take(packed, tile_sets, axis=0)
    cuts = [sum(sizes[:i]) for i in range(len(sizes) + 1)]

    def piece(i, shape):
        return picked[:, cuts[i] : cuts[i + 1]].reshape((tiles,) + shape)

    t_qkv_a = piece(0, (3, RANK, full_width))
    t_qkv_b = piece(1, (3, RANK, local_width))
    t_out_a = piece(2, (RANK, local_width))
    t_out_b = piece(3, (RANK, full_width))
    t_router_a = piece(4, (RANK, full_width))
    t_router_b = picked[:, cuts[5], : RANK * EXPERTS].reshape(tiles, RANK, EXPERTS)

    token_vals = tokens.astype(f32)
    cot_vals = cotangent.astype(f32)
    gain_in = norm_in.astype(f32)
    gain_mid = norm_mid.astype(f32)
    gain_q = q_gain.astype(f32)
    gain_k = k_gain.astype(f32)
    first_scale = lax.rsqrt(jnp.mean(token_vals * token_vals, axis=1, keepdims=True) + epsilon)
    h_first = (token_vals * first_scale * gain_in).astype(bf16)

    def exchange(x, bits, beside=None):
        blocks = {0: x}
        for bit in bits:
            names = sorted(blocks)
            sent = jnp.stack([blocks[i] for i in names])
            if bit == bits[-1] and beside is not None:
                sent, beside = lax.optimization_barrier((sent, beside))
            got = across(sent, bit)
            blocks.update({i ^ bit: got[at] for at, i in enumerate(names)})
        return [blocks[i] for i in range(slab_count)], beside

    half_n = shard_count // 2
    near_at = jnp.bitwise_xor(jnp.arange(slab_count, dtype=jnp.int32), slab_index)[None, :]
    step_at = ((shard_at - shard_index) % shard_count)[:, None]
    row_at = (step_at // half_n) * (half_n * slab_count) + near_at * half_n + step_at % half_n
    row_at = row_at.reshape(-1)

    def fetch(x):
        mine = my_slab(x, 0)
        return [mine] + [from_shard(mine, s) for s in range(1, shard_count)]

    def spread(got, beside=None):
        near, beside = exchange(jnp.stack(got[:half_n]), slab_bits, beside)
        far, beside = exchange(jnp.stack(got[half_n:]), slab_bits[::-1], beside)
        return jnp.concatenate(near + far, axis=0), beside

    got_k = fetch(w_qkv[:, 1])
    got_k, w_v, w_q = lax.optimization_barrier((got_k, w_qkv[:, 2], w_qkv[:, 0]))
    got_v = fetch(w_v)
    got_v, w_q = lax.optimization_barrier((got_v, w_q))
    got_q = fetch(w_q)
    got_q, w_out, cot_mine, gu_a, gu_b, down_a, down_b = lax.optimization_barrier(
        (got_q, w_out, my_part(cotangent), gu_a, gu_b, down_a, down_b)
    )
    def experts_of_sets(x, axes):
        count, width_x = lax.axis_size(axes), x.shape[3]
        x = x.reshape(sets_local, shard_count, -1, width_x).transpose(1, 0, 2, 3)
        x = x.reshape(shard_count, count, -1, width_x)
        got = []
        for s in range(shard_count):
            at = ((shard_index - s) % shard_count, lax.axis_index(axes), 0, 0)
            block = lax.dynamic_slice(x, at, (1, 1) + x.shape[2:])[0, 0]
            got.append(from_shard(block, s) if s else block)
        return jnp.stack(got)

    def gather_adapters(x, axes):
        whole = lax.all_gather(x, axes, axis=1, tiled=True)
        return whole.reshape(SETS, -1, x.shape[2])

    def scatter_experts(x, axes):
        x = x.astype(bf16).reshape(shard_count, -1, x.shape[2])
        return lax.psum_scatter(x, axes, scatter_dimension=1, tiled=True)

    def sets_of_experts(mine, axes):
        width_x = mine.shape[2]
        got = [to_shard(mine[s], s) if s else mine[s] for s in range(shard_count)]
        whole = lax.all_gather(by_shard(got, shard_index - shard_at), axes, axis=1, tiled=True)
        return whole.reshape(shard_count, sets_local, locals_n, -1, width_x).transpose(1, 0, 2, 3, 4)

    wide = jnp.concatenate(
        [gu_a.transpose(0, 1, 3, 4, 2).reshape(sets_local, EXPERTS, -1, full_width), down_b], axis=2
    )
    slim = jnp.concatenate(
        [
            gu_b.transpose(0, 1, 3, 2, 4).reshape(sets_local, EXPERTS, -1, ff_local),
            down_a.transpose(0, 1, 3, 2),
        ],
        axis=2,
    )
    wide = experts_of_sets(wide, ("ctx", "tp"))
    slim = experts_of_sets(slim, ("ctx",))
    w_gu = w_gate_up.transpose(0, 2, 1, 3)
    sums = tuple(
        jnp.zeros((SETS, 3 * RANK * locals_n, x), f32) for x in (full_width, ff_local)
    )
    blocks_k, _ = spread(got_k)
    blocks_v, _ = spread(got_v)
    blocks_q, (wide, slim, w_gu) = spread(got_q, (wide, slim, w_gu))
    cot_mine, wide = lax.optimization_barrier((cot_mine, wide))
    cot_near = from_shard(cot_mine, 1)
    blocks_q, cot_near, sums = lax.optimization_barrier((blocks_q, cot_near, sums))
    weights = jnp.take(jnp.stack([blocks_q, blocks_k, blocks_v]), row_at, axis=1).reshape(
        3, full_width, local_width
    )
    cot_mine, cot_near = lax.optimization_barrier((cot_mine, cot_near))
    cot_last = from_shard(cot_mine, shard_count - 1)
    cot_rest = [from_shard(cot_mine, s) for s in range(2, shard_count - 1)]
    mid_qkv = (
        ADAPTER_SCALE
        * jnp.einsum("tnd,tjrd->tnjr", tile_rows(h_first), t_qkv_a, preferred_element_type=f32)
    ).astype(bf16)

    def project(j):
        return jnp.dot(h_first, weights[j], preferred_element_type=f32) + jnp.einsum(
            "tnr,tro->tno", mid_qkv[:, :, j], t_qkv_b[:, j], preferred_element_type=f32
        ).reshape(row_count, local_width)

    def scale_of(raw):
        squares = sum_parts(jnp.sum(raw * raw, axis=1))
        return lax.rsqrt(squares / full_width + epsilon)[:, None]

    k_raw = project(1)
    k_scale = scale_of(k_raw)
    value_rows = project(2).astype(bf16)
    q_raw = project(0)
    q_scale = scale_of(q_raw)

    def heads_of(x):
        return x.reshape(x.shape[0], local_heads, HEAD_DIM)

    query_rows = (
        rotate(heads_of(q_raw * q_scale * gain_q), cosine, sine_part)
        .reshape(row_count, local_width)
        .astype(bf16)
    )
    key_rows = (
        rotate(heads_of(k_raw * k_scale * gain_k), cosine, sine_part)
        .reshape(row_count, local_width)
        .astype(bf16)
    )

    def exchange_back(x, bits, beside=None):
        blocks = {i: x[i * prompt_rows : (i + 1) * prompt_rows] for i in range(slab_count)}
        for bit in bits:
            sent = sorted(i for i in blocks if i & bit)
            rows_ = jnp.stack([blocks[i].astype(bf16) for i in sent])
            if bit == bits[-1] and beside is not None:
                rows_, beside = lax.optimization_barrier((rows_, beside))
            got = across(rows_, bit)
            for at, i in enumerate(sent):
                blocks[i ^ bit] = blocks[i ^ bit].astype(f32) + got[at].astype(f32)
                del blocks[i]
        return blocks[0], beside

    prompt_values, _ = exchange(value_rows[:prompt_rows], slab_bits[::-1])
    prompt_keys, cot_last = exchange(key_rows[:prompt_rows], slab_bits, cot_last)
    prompt_keys = jnp.concatenate(prompt_keys, axis=0)
    prompt_values = jnp.concatenate(prompt_values, axis=0)
    key_own, value_own = key_rows[prompt_rows:], value_rows[prompt_rows:]
    wide = gather_adapters(wide, ("ctx", "tp"))
    slim = gather_adapters(slim, ("ctx",))
    attention_rows, log_total = attention_forward(
        slab, query_rows, prompt_keys, prompt_values, key_own, value_own, prompt_rows
    )
    attention_rows, cot_rest, wide, slim = lax.optimization_barrier(
        (attention_rows, cot_rest, wide, slim)
    )
    cot_got = [cot_near] + cot_rest + [cot_last]
    whole_out = lax.all_gather(my_slab(w_out, 1), ("fsdp", "ctx"), axis=1, tiled=True)
    mid_out = (
        ADAPTER_SCALE
        * jnp.einsum("tnd,trd->tnr", tile_rows(attention_rows), t_out_a, preferred_element_type=f32)
    ).astype(bf16)
    branch = sum_parts(
        jnp.dot(attention_rows, whole_out, preferred_element_type=f32)
        + jnp.einsum("tnr,trd->tnd", mid_out, t_out_b, preferred_element_type=f32).reshape(
            row_count, full_width
        )
    )
    x_mid = token_vals + branch
    mid_scale = lax.rsqrt(jnp.mean(x_mid * x_mid, axis=1, keepdims=True) + epsilon)
    h_second = (x_mid * mid_scale * gain_mid).astype(bf16)
    h_tiles = tile_rows(h_second)
    mid_router = (
        ADAPTER_SCALE
        * jnp.einsum("tnd,trd->tnr", h_tiles, t_router_a, preferred_element_type=f32)
    ).astype(bf16)
    router_logits = jnp.dot(h_second, w_router, preferred_element_type=f32) + jnp.einsum(
        "tnr,tre->tne", mid_router, t_router_b, preferred_element_type=f32
    ).reshape(row_count, EXPERTS)
    expert_probs = jax.nn.softmax(router_logits, axis=1)
    chosen = jnp.any(
        routes[:, :, None] == jnp.arange(EXPERTS, dtype=jnp.int32)[None, None, :], axis=1
    )
    gates = jnp.where(chosen, expert_probs, 0.0)

    gu_rank = 2 * RANK
    adapters = (wide, slim)
    part = part_index.reshape(1).astype(jnp.int32)
    h_mine = my_part(h_second)
    cot_steps = [cotangent] + [(x, swap(x)) for x in cot_got]
    gates_t = gates.T
    gate_steps = []
    for s in range(shard_count):
        block = lax.dynamic_slice_in_dim(
            gates_t, ((shard_index - s) % shard_count) * locals_n, locals_n, axis=0
        )
        gate_steps.append((from_shard(block, s) if s else block).T)
    h_mine, gate_steps = lax.optimization_barrier((h_mine, gate_steps))
    y_steps, dh_steps, d_gate_steps = [], [], []
    h_step = h_second
    h_next = from_shard(h_mine, 1)
    for s in range(shard_count):
        y_keep, y_send, dh_keep, dh_send, d_gate, *sums = expert_pass(
            step_order[s], step_order_sets[s], part, h_step, cot_steps[s], gate_steps[s], w_gu,
            w_down, adapters, tuple(sums),
        )
        last = s + 1 == shard_count
        d_gate = d_gate.T
        dh_send, d_gate, dh_steps, h_next = lax.optimization_barrier(
            (dh_send, d_gate, dh_steps, h_next)
        )
        d_gate = to_shard(d_gate, s) if s else d_gate
        dh = dh_keep.astype(f32) + swap(dh_send).astype(f32)
        dh = dh.astype(bf16) if s else dh
        if not last:
            h_step = (h_next, swap(h_next))
        sums, h_step, h_mine, dh, d_gate = lax.optimization_barrier(
            (sums, h_step, h_mine, dh, d_gate)
        )
        if s + 2 < shard_count:
            h_next = from_shard(h_mine, s + 2)
        dh_steps.append(to_shard(dh, s) if s else dh)
        d_gate_steps.append(d_gate)
        y_steps.append((y_keep, y_send))
    d_gates = sum_parts(
        by_shard(d_gate_steps, shard_index - shard_at).reshape(EXPERTS, row_count)
    ).T
    d_second_mine = sum(dh.astype(f32) for dh in dh_steps).astype(bf16)
    y_steps = [keep.astype(f32) + swap(send).astype(f32) for keep, send in y_steps]
    y_steps = [y.astype(bf16) if s else y for s, y in enumerate(y_steps)]
    d_second_mine, y_steps, sums = lax.optimization_barrier((d_second_mine, y_steps, sums))
    wide_mine = scatter_experts(sums[0], ("ctx", "tp"))
    slim_mine = scatter_experts(sums[1], ("ctx",))
    d_second_routed = join_parts(d_second_mine, swap(d_second_mine)).astype(f32)
    y_first = [to_shard(y_steps[s], s) for s in range(1, shard_count - 1)]

    d_probs = jnp.where(chosen, d_gates, 0.0)
    d_logits = (
        expert_probs * (d_probs - jnp.sum(expert_probs * d_probs, axis=1, keepdims=True))
    ).astype(bf16)
    dl_tiles = tile_rows(d_logits)
    d_mid_router = (
        ADAPTER_SCALE
        * jnp.einsum("tne,tre->tnr", dl_tiles, t_router_b, preferred_element_type=f32)
    ).astype(bf16)
    g_router_b = jnp.einsum("tnr,tne->tre", mid_router, dl_tiles, preferred_element_type=f32)
    g_router_a = jnp.einsum("tnr,tnd->trd", d_mid_router, h_tiles, preferred_element_type=f32)
    d_second = (
        d_second_routed
        + jnp.einsum("ne,de->nd", d_logits, w_router, preferred_element_type=f32)
        + jnp.einsum("tnr,trd->tnd", d_mid_router, t_router_a, preferred_element_type=f32).reshape(
            row_count, full_width
        )
    )
    d_x_mid = cot_vals + rms_back(x_mid, gain_mid, d_second, mid_scale, full_width)
    d_branch = d_x_mid.astype(bf16)
    db_tiles = tile_rows(d_branch)
    d_mid_out = (
        ADAPTER_SCALE
        * jnp.einsum("tnd,trd->tnr", db_tiles, t_out_b, preferred_element_type=f32)
    ).astype(bf16)
    d_att = jnp.einsum("nc,oc->no", d_branch, whole_out, preferred_element_type=f32) + jnp.einsum(
        "tnr,tro->tno", d_mid_out, t_out_a, preferred_element_type=f32
    ).reshape(row_count, local_width)
    g_out_b = jnp.einsum("tnr,tnd->trd", mid_out, db_tiles, preferred_element_type=f32)
    g_out_a = jnp.einsum(
        "tnr,tno->tro", d_mid_out, tile_rows(attention_rows), preferred_element_type=f32
    )
    d_att_rows = d_att.astype(bf16)
    d_query, d_key_all, d_value_all, d_key_own, d_value_own = attention_backward(
        slab, query_rows, prompt_keys, prompt_values, key_own, value_own, attention_rows,
        d_att_rows, log_total, prompt_rows,
    )
    d_key_all, d_value_all, y_first, y_last = lax.optimization_barrier(
        (d_key_all, d_value_all, y_first, y_steps[-1])
    )
    y_last = to_shard(y_last, shard_count - 1)
    d_key_prompt, y_last = exchange_back(d_key_all, slab_bits, y_last)
    d_value_prompt, _ = exchange_back(d_value_all, slab_bits[::-1])
    d_key_prompt, wide_mine, slim_mine = lax.optimization_barrier(
        (d_key_prompt, wide_mine, slim_mine)
    )
    g_wide = sets_of_experts(wide_mine, ("ctx", "tp"))
    g_slim = sets_of_experts(slim_mine, ("ctx",))
    d_key = jnp.concatenate([d_key_prompt, d_key_own], axis=0)
    d_value = jnp.concatenate([d_value_prompt, d_value_own], axis=0)
    d_q_norm = rotate(heads_of(d_query), cosine, -sine_part).reshape(row_count, local_width)
    d_k_norm = rotate(heads_of(d_key), cosine, -sine_part).reshape(row_count, local_width)
    dots = sum_parts(
        jnp.stack(
            [jnp.sum(gain_q * q_raw * d_q_norm, axis=1), jnp.sum(gain_k * k_raw * d_k_norm, axis=1)]
        )
    )
    d_q_raw = (
        q_scale * gain_q * d_q_norm
        - q_raw * (q_scale * q_scale * q_scale) * dots[0][:, None] / full_width
    )
    d_k_raw = (
        k_scale * gain_k * d_k_norm
        - k_raw * (k_scale * k_scale * k_scale) * dots[1][:, None] / full_width
    )
    d_proj = jnp.stack([d_q_raw, d_k_raw, d_value], axis=0).astype(bf16)
    mixed_mine = sum(
        [y.astype(f32) for y in [y_steps[0], *y_first, y_last]], my_part(x_mid)
    ).astype(bf16)
    mixed = join_parts(mixed_mine, swap(mixed_mine))
    dp_tiles = d_proj.reshape(3, tiles, TILE, local_width)
    d_mid_qkv = (
        ADAPTER_SCALE
        * jnp.einsum("jtno,tjro->tnjr", dp_tiles, t_qkv_b, preferred_element_type=f32)
    ).astype(bf16)
    d_first = sum_parts(
        jnp.einsum("jno,jdo->nd", d_proj, weights, preferred_element_type=f32)
        + jnp.einsum("tnjr,tjrd->tnd", d_mid_qkv, t_qkv_a, preferred_element_type=f32).reshape(
            row_count, full_width
        )
    )
    d_first, g_wide, g_slim = lax.optimization_barrier((d_first, g_wide, g_slim))
    grad_input = d_x_mid + rms_back(token_vals, gain_in, d_first, first_scale, full_width)
    g_qkv_b = jnp.einsum("tnjr,jtno->tjro", mid_qkv, dp_tiles, preferred_element_type=f32)
    g_qkv_a = jnp.einsum(
        "tnjr,tnd->tjrd", d_mid_qkv, tile_rows(h_first), preferred_element_type=f32
    )

    def to_sets(pieces_):
        rows_ = jnp.concatenate(pieces_, axis=1)
        return jnp.sum(tile_hot[:, :, None, None] * rows_[None], axis=1).astype(bf16)

    def both_parts(x):
        return (x.astype(f32) + swap(x).astype(f32)).astype(bf16)

    def add(mine, other):
        return (mine.astype(f32) + other.astype(f32)).astype(bf16)

    def reduced(x):
        n_rows, half_width = x.shape[1], local_width // 2
        x = jnp.pad(x, ((0, 0), (0, -n_rows % (16 * slab_count)), (0, 0)))
        halves = []
        for i, bits in enumerate((slab_bits, slab_bits[::-1])):
            y = x[:, :, i * half_width : (i + 1) * half_width]
            for bit in bits:
                high = (slab_index // bit) % 2
                y = y.reshape(y.shape[0], 2, y.shape[1] // 2, half_width)
                y = add(
                    lax.dynamic_index_in_dim(y, high, axis=1, keepdims=False),
                    across(lax.dynamic_index_in_dim(y, 1 - high, axis=1, keepdims=False), bit),
                )
            y = y.reshape(shard_count, sets_local, y.shape[1], half_width)
            blocks = []
            for s in range(shard_count):
                block = lax.dynamic_index_in_dim(
                    y, (shard_index + s) % shard_count, axis=0, keepdims=False
                )
                blocks.append(to_shard(block, s) if s else block)
            y = sum(block.astype(f32) for block in blocks).astype(bf16)
            for bit in bits[::-1]:
                is_high = (slab_index // bit) % 2 == 1
                other = across(y, bit)
                y = jnp.concatenate(
                    [jnp.where(is_high, other, y), jnp.where(is_high, y, other)], axis=1
                )
            halves.append(y)
        return jnp.concatenate(halves, axis=2)[:, :n_rows].astype(f32)

    summed = reduced(
        jnp.concatenate(
            [
                both_parts(to_sets([as_rows(g_qkv_a), as_rows(g_out_b)])),
                to_sets([as_rows(g_qkv_b), as_rows(g_out_a), as_rows(g_router_a)]),
                to_sets([router_rows(g_router_b)]),
            ],
            axis=1,
        )
    )
    order_ = (sizes[0], sizes[3], sizes[1], sizes[2], sizes[4], sizes[5])
    cuts = [sum(order_[:i]) for i in range(len(order_) + 1)]
    s_qkv_a, s_out_b, s_qkv_b, s_out_a, s_router_a, s_router_b = [
        summed[:, cuts[i] : cuts[i + 1]] for i in range(len(order_))
    ]
    grad_qkv_a = s_qkv_a.reshape(sets_local, 3, RANK, full_width).transpose(0, 3, 1, 2)
    grad_qkv_b = s_qkv_b.reshape(sets_local, 3, RANK, local_width).transpose(0, 2, 1, 3)
    grad_out_b = s_out_b.reshape(out_b.shape)
    grad_out_a = s_out_a.reshape(sets_local, RANK, local_width).transpose(0, 2, 1)
    grad_router_a = s_router_a.reshape(sets_local, RANK, full_width).transpose(0, 2, 1)
    grad_router_b = s_router_b[:, 0, : RANK * EXPERTS].reshape(router_b.shape)

    def of_experts(g):
        return g.reshape((sets_local, EXPERTS) + g.shape[3:]).astype(f32)

    grad_gu_a = (
        of_experts(g_wide[:, :, :, :gu_rank])
        .reshape(sets_local, EXPERTS, 2, RANK, full_width)
        .transpose(0, 1, 4, 2, 3)
    )
    grad_gu_b = (
        of_experts(g_slim[:, :, :, :gu_rank])
        .reshape(sets_local, EXPERTS, 2, RANK, ff_local)
        .transpose(0, 1, 3, 2, 4)
    )
    grad_down_a = of_experts(g_slim[:, :, :, gu_rank:]).transpose(0, 1, 3, 2)
    grad_down_b = of_experts(g_wide[:, :, :, gu_rank:])
    return (
        mixed, grad_input, grad_qkv_a, grad_qkv_b, grad_out_a, grad_out_b, grad_router_a,
        grad_router_b, grad_gu_a, grad_gu_b, grad_down_a, grad_down_b,
    )


def solution(mesh):
    return jax.shard_map(
        per_device,
        mesh=mesh,
        in_specs=(
            P(("fsdp", "ctx"), None),
            P(("fsdp", "ctx"), None),
            P(("fsdp", "ctx"), None),
            P("fsdp", None),
            P(),
            P(),
            P("tp"),
            P("tp"),
            P("fsdp", None, "tp"),
            P("tp", "fsdp"),
            P(),
            P("fsdp", None, None, "tp"),
            P("fsdp", "tp", None),
            P("fsdp", None, None, None),
            P("fsdp", None, None, "tp"),
            P("fsdp", "tp", None),
            P("fsdp", None, None),
            P("fsdp", None, None),
            P("fsdp", None, None),
            P("fsdp", None, None, None, None),
            P("fsdp", None, None, None, "tp"),
            P("fsdp", None, "tp", None),
            P("fsdp", None, None, None),
        ),
        out_specs=(
            P(("fsdp", "ctx"), None),
            P(("fsdp", "ctx"), None),
            P("fsdp", None, None, None),
            P("fsdp", None, None, "tp"),
            P("fsdp", "tp", None),
            P("fsdp", None, None),
            P("fsdp", None, None),
            P("fsdp", None, None),
            P("fsdp", None, None, None, None),
            P("fsdp", None, None, None, "tp"),
            P("fsdp", None, "tp", None),
            P("fsdp", None, None, None),
        ),
        check_vma=False,
    )
```
